512 devices in a mesh: sen: 32 (over y, z_hi), par: 16 (over x, z_lo, core).
Axes of the slice: x: 4, y: 8, z: 8 (z_hi: 4, z_lo: 2; z = z_hi * 2 + z_lo), core: 2. Of those that a mesh axis runs over, the one named last changes fastest.
Arguments:
- vectors: float32 [2, 256, 256], P(None, 'sen'), may hold values from -6 to 6
- observed: float32 [2, 256, 256], P(None, 'sen'), may hold values from -6 to 6
- operator: bfloat16 [2, 128, 256, 6144], P(None, None, 'sen', 'par'), may hold values from -0.15625 to 0.15625
- noise: float32 [256], P('sen'), may hold values from 0.3 to 3
- coefficient: float32 [16, 384], P('par'), may hold values from 0.05 to 0.24
- offsets: int32 [16, 384], P('par'), may hold values from -3 to 3
Outputs:
- residual: float32 [2, 256, 256], P(None, 'sen')
- applied: float32 [2, 256, 256], P(None, 'sen')
The draws below stay inside these ranges and needn't reach their ends.
All inputs are finite; a program needn't handle non-finite values.
Results may differ from the reference program's by a relative error of at most 0.0018.
Values may be sent and summed in bfloat16 or wider, within the bound.
A program may use at most 64 MiB of HBM per device.

```python
import math
import jax
import jax.numpy as jnp
from jax import lax

NT = 256
NF = 128
RHS = 2
SWEEPS = 4
GY = 384
NS = 256
GX = 16
NP = 6144


def plant(values, stream_key, least, largest):
    place = [jax.random.randint(jax.random.fold_in(stream_key, axis), (), 0, length) for axis, length in enumerate(values.shape)]
    main_axis = values.shape.index(max(values.shape))
    beside = place[:main_axis] + [(place[main_axis] + 1) % values.shape[main_axis]] + place[main_axis + 1:]
    return values.at[tuple(place)].set(least).at[tuple(beside)].set(largest)


def levels(own_key, dims, shards, least, high):
    factor_of, own = 1.0, jax.random.fold_in(own_key, 6)
    for dim, parts in shards:
        draws = jnp.exp(jax.random.uniform(jax.random.fold_in(own, dim), (parts,), jnp.float32, least / len(shards), high / len(shards)))
        factor_of = factor_of * jnp.repeat(draws, dims[dim] // parts).reshape([-1 if axis == dim else 1 for axis in range(len(dims))])
    return factor_of


def centred(own_key, dims, spread, most, split=(), kind=jnp.bfloat16):
    entries = spread * jax.random.normal(own_key, dims, jnp.float32)
    if split:
        entries = entries * levels(own_key, dims, split, -0.22, 0.18)
    return jnp.clip(entries, -most, most).astype(kind)


def setup_inputs(seed: int = 0) -> dict:
    arg_keys = jax.random.split(jax.random.key(seed), 7)
    return {
        "vectors": centred(arg_keys[0], (RHS, NS, NT), 1.0, 6.0, ((1, 32),), jnp.float32),
        "observed": centred(arg_keys[1], (RHS, NS, NT), 1.0, 6.0, ((1, 32),), jnp.float32),
        "operator": centred(arg_keys[2], (2, NF, NS, NP), (NP // 4) ** -0.5, 0.15625, ((2, 32), (3, 16))),
        "noise": jnp.clip(jnp.exp(math.log(3.0) - 2.3025851 * jax.random.uniform(arg_keys[3], (NS,), jnp.float32) ** levels(arg_keys[3], (NS,), ((0, 32),), -0.2, 0.2)), 0.3, 3.0),
        "coefficient": jnp.clip(0.05 + 0.19 * jax.random.uniform(arg_keys[4], (GX, GY), jnp.float32) ** levels(arg_keys[4], (GX, GY), ((0, 16),), -0.2, 0.2), 0.05, 0.24),
        "offsets": plant(jax.random.randint(arg_keys[5], (GX, GY), -3, 4), jax.random.fold_in(arg_keys[5], 1), -3, 3).astype(jnp.int32),
    }


def make_basis(length):
    half = length // 2
    times = jnp.arange(length, dtype=jnp.int32)[:, None]
    freqs = jnp.arange(half, dtype=jnp.int32)[None, :]
    phase = (2 * freqs + 1) * times % (2 * length)
    angle = phase.astype(jnp.float32) * (math.pi / length)
    scale = math.sqrt(2.0 / length)
    return jnp.concatenate([jnp.cos(angle), jnp.sin(angle)], axis=1) * scale

def smooth(field, coefficient, offsets):
    width = field.shape[-1]
    for sweep in range(SWEEPS):
        padded = jnp.pad(field, ((0, 0), (0, 0), (0, 0), (1, 1), (0, 0)))
        upper = padded[..., :-2, :]
        lower = padded[..., 2:, :]
        lower_pad = jnp.pad(lower, ((0, 0), (0, 0), (0, 0), (0, 0), (3, 3)))
        linked = jnp.zeros_like(field)
        for shift in range(-3, 4):
            linked = linked + jnp.where(offsets == shift, lower_pad[..., 3 + shift:3 + shift + width], 0.0)
        sides = jnp.pad(field, ((0, 0), (0, 0), (0, 0), (0, 0), (1, 1)))
        field = field + coefficient * (sides[..., :-2] + sides[..., 2:] + upper + linked - 4.0 * field)
    return field

def hessian(record, operator, noise, coefficient, offsets, basis):
    rows, sensors, length = record.shape
    half = length // 2
    spectrum = jnp.dot(record.reshape(rows * sensors, length), basis, precision=lax.Precision.HIGHEST)
    spectrum = spectrum.reshape(rows, sensors, 2, half).transpose(2, 3, 0, 1).astype(jnp.bfloat16)

    def adjoint_one(freq):
        resp = lax.dynamic_index_in_dim(operator, freq, 1, keepdims=False)
        spec = lax.dynamic_index_in_dim(spectrum, freq, 1, keepdims=False)
        real = jnp.dot(spec[0], resp[0], preferred_element_type=jnp.float32) + jnp.dot(spec[1], resp[1], preferred_element_type=jnp.float32)
        imag = jnp.dot(spec[1], resp[0], preferred_element_type=jnp.float32) - jnp.dot(spec[0], resp[1], preferred_element_type=jnp.float32)
        return jnp.stack([real, imag])
    adjoint = lax.map(adjoint_one, jnp.arange(half, dtype=jnp.int32))
    cells = adjoint.shape[-1]
    field = jnp.moveaxis(adjoint, 0, 1).reshape(2, half, rows, cells // GY, GY)
    prior = smooth(field, coefficient, offsets).astype(jnp.bfloat16).reshape(2, half, rows, cells)

    def forward_one(freq):
        resp = lax.dynamic_index_in_dim(operator, freq, 1, keepdims=False)
        par = lax.dynamic_index_in_dim(prior, freq, 1, keepdims=False)
        real = jnp.dot(par[0], resp[0].T, preferred_element_type=jnp.float32) - jnp.dot(par[1], resp[1].T, preferred_element_type=jnp.float32)
        imag = jnp.dot(par[1], resp[0].T, preferred_element_type=jnp.float32) + jnp.dot(par[0], resp[1].T, preferred_element_type=jnp.float32)
        return jnp.stack([real, imag])
    forward = lax.map(forward_one, jnp.arange(half, dtype=jnp.int32))
    forward = forward.transpose(2, 3, 1, 0).reshape(rows * sensors, length)
    back = jnp.dot(forward, basis.T, precision=lax.Precision.HIGHEST).reshape(rows, sensors, length)
    return back + noise[None, :, None] * record

def reference(vectors, observed, operator, noise, coefficient, offsets):
    basis = make_basis(vectors.shape[-1])
    residual = observed - hessian(vectors, operator, noise, coefficient, offsets, basis)
    applied = hessian(residual, operator, noise, coefficient, offsets, basis)
    return (residual, applied)
```

```python
import math

import jax
import jax.numpy as jnp
from jax import lax
from jax.sharding import PartitionSpec as P

SWEEPS = 4


def make_basis(length):
    half = length // 2
    times = jnp.arange(length, dtype=jnp.int32)[:, None]
    freqs = jnp.arange(half, dtype=jnp.int32)[None, :]
    phase = (2 * freqs + 1) * times % (2 * length)
    angle = phase.astype(jnp.float32) * (math.pi / length)
    scale = math.sqrt(2.0 / length)
    return jnp.concatenate([jnp.cos(angle), jnp.sin(angle)], axis=1) * scale


def smooth(field, coefficient, offsets):
    width = field.shape[-1]
    for sweep in range(SWEEPS):
        padded = jnp.pad(field, ((1, 1), (0, 0)))
        upper = padded[:-2]
        lower_pad = jnp.pad(padded[2:], ((0, 0), (3, 3)))
        linked = jnp.zeros_like(field)
        for shift in range(-3, 4):
            linked = linked + jnp.where(
                offsets == shift, lower_pad[:, 3 + shift : 3 + shift + width], 0.0
            )
        sides = jnp.pad(field, ((0, 0), (1, 1)))
        field = field + coefficient * (sides[:, :-2] + sides[:, 2:] + upper + linked - 4.0 * field)
    return field


def hessian(record, operator, noise, coefficient, offsets, basis):
    rows, sensors, length = record.shape
    half = length // 2
    cells = operator.shape[-1]
    spectrum = jnp.dot(
        record.reshape(rows * sensors, length), basis, precision=lax.Precision.HIGHEST
    )
    spectrum = spectrum.reshape(rows, sensors, 2, half).transpose(2, 3, 0, 1).astype(jnp.bfloat16)
    real = jnp.einsum(
        "frs,fsp->frp", spectrum[0], operator[0], preferred_element_type=jnp.float32
    ) + jnp.einsum("frs,fsp->frp", spectrum[1], operator[1], preferred_element_type=jnp.float32)
    imag = jnp.einsum(
        "frs,fsp->frp", spectrum[1], operator[0], preferred_element_type=jnp.float32
    ) - jnp.einsum("frs,fsp->frp", spectrum[0], operator[1], preferred_element_type=jnp.float32)
    planes = jnp.stack([real, imag], axis=1).reshape(half * 2 * rows, cells)
    planes = lax.psum_scatter(planes, "sen", scatter_dimension=0, tiled=True)
    plane = lax.all_to_all(planes, "par", 0, 0, tiled=True)
    prior = smooth(plane, coefficient, offsets).astype(jnp.bfloat16)
    planes = lax.all_to_all(prior, "par", 0, 0, tiled=True)
    planes = lax.all_gather(planes, "sen", axis=0, tiled=True)
    planes = planes.reshape(half, 2, rows, cells)
    flat = (planes[:, 0], planes[:, 1])
    real = jnp.einsum(
        "fsp,frp->frs", operator[0], flat[0], preferred_element_type=jnp.float32
    ) - jnp.einsum("fsp,frp->frs", operator[1], flat[1], preferred_element_type=jnp.float32)
    imag = jnp.einsum(
        "fsp,frp->frs", operator[0], flat[1], preferred_element_type=jnp.float32
    ) + jnp.einsum("fsp,frp->frs", operator[1], flat[0], preferred_element_type=jnp.float32)
    forward = lax.psum(jnp.stack([real, imag]), "par")
    forward = forward.transpose(2, 3, 0, 1).reshape(rows * sensors, length)
    back = jnp.dot(forward, basis.T, precision=lax.Precision.HIGHEST).reshape(rows, sensors, length)
    return back + noise[None, :, None] * record


def body(vectors, observed, operator, noise, coefficient, offsets):
    basis = make_basis(vectors.shape[-1])
    coefficient = lax.all_gather(coefficient, "par", axis=0, tiled=True)
    offsets = lax.all_gather(offsets, "par", axis=0, tiled=True)
    residual = observed - hessian(vectors, operator, noise, coefficient, offsets, basis)
    applied = hessian(residual, operator, noise, coefficient, offsets, basis)
    return (residual, applied)


def solution(mesh):
    placed = (
        P(None, "sen", None),
        P(None, "sen", None),
        P(None, None, "sen", "par"),
        P("sen"),
        P("par", None),
        P("par", None),
    )
    return jax.shard_map(
        body,
        mesh=mesh,
        in_specs=placed,
        out_specs=(P(None, "sen", None), P(None, "sen", None)),
        check_vma=False,
    )
```

```python
import math

import jax
import jax.numpy as jnp
import numpy as np
from jax import lax
from jax.experimental import pallas as pl
from jax.experimental.pallas import tpu as pltpu
from jax.sharding import PartitionSpec as P

SWEEPS = 4
NY, NZH, NX, NZL = 8, 4, 4, 2
NZ = NZH * NZL
SLAB = NY * NZ * 2
F32, BF16 = jnp.float32, jnp.bfloat16


def basis_rows(length):
    half = length // 2
    freqs = np.arange(half)[:, None]
    times = np.arange(length)[None, :]
    angle = ((2 * freqs + 1) * times % (2 * length)) * (math.pi / length)
    scale = math.sqrt(2.0 / length)
    return np.concatenate([np.cos(angle) * scale, np.sin(angle) * scale], 1).astype(np.float32)


def dot_rows(a, b, **kw):
    return lax.dot_general(a, b, (((1,), (1,)), ((), ())), preferred_element_type=F32, **kw)


def kernel(
    vec_ref, obs_ref, op_ref, noise_ref, coef_ref, offs_ref, basis_ref,
    res_ref, app_ref,
    w_buf, spec_own, spec_buf, co_buf, halo, sums, out_own, out_buf,
    op_send, op_recv, op_local, spec_send, spec_recv, row_send, row_recv, co_send, co_recv,
    halo_send, halo_recv, sum_send, sum_recv, out_send, out_recv,
):
    sen = lax.axis_index("sen")
    par = lax.axis_index("par")
    y, zh = lax.div(sen, NZH), lax.rem(sen, NZH)
    x, q_me = lax.div(par, 4), lax.rem(par, 4)
    zl, c = lax.div(q_me, 2), lax.rem(q_me, 2)
    z = zh * NZL + zl
    f_me = (y * NZ + z) * 2 + c

    def peer(k):
        dy = lax.rem(k, NY)
        dz = lax.rem(lax.div(k, NY) + 3 * dy, NZ)
        dc = lax.div(k, NY * NZ)
        y2 = lax.rem(y + dy, NY)
        z2 = lax.rem(z + dz, NZ)
        c2 = lax.rem(c + dc, 2)
        sen2 = y2 * NZH + lax.div(z2, NZL)
        par2 = x * 4 + lax.rem(z2, NZL) * 2 + c2
        return (y2 * NZ + z2) * 2 + c2, dc, sen2, par2

    def at(sen2, par2):
        return {"sen": sen2, "par": par2}

    def in_x(dx):
        return at(sen, lax.rem(x + dx, NX) * 4 + q_me)

    def remote(src, dst, send, recv, device):
        copy = pltpu.make_async_remote_copy(
            src_ref=src, dst_ref=dst, send_sem=send, recv_sem=recv,
            device_id=device, device_id_type=pl.DeviceIdType.MESH,
        )
        copy.start()

    def take(ref, sem):
        pltpu.make_async_copy(ref, ref, sem).wait()

    barrier = pltpu.get_barrier_semaphore()

    def greet(k, carry):
        _, _, sen2, par2 = peer(k)
        pl.semaphore_signal(barrier, inc=1, device_id=at(sen2, par2), device_id_type=pl.DeviceIdType.MESH)
        return carry

    lax.fori_loop(1, SLAB, greet, 0)
    for dx in range(1, NX):
        pl.semaphore_signal(barrier, inc=1, device_id=in_x(dx), device_id_type=pl.DeviceIdType.MESH)

    own_op = pltpu.make_async_copy(op_ref.at[:, f_me], w_buf.at[c, zl, :, sen], op_local)
    own_op.start()

    eye = lax.broadcasted_iota(jnp.int32, (8, 8), 0) == lax.broadcasted_iota(jnp.int32, (8, 8), 1)
    noise = jnp.sum(jnp.where(eye, noise_ref[...], 0.0), axis=1, keepdims=True)
    noise16 = jnp.concatenate([noise, noise], axis=0)
    vec = vec_ref[...].reshape(16, 256)
    rest = obs_ref[...].reshape(16, 256) - noise16 * vec
    record = jnp.concatenate([vec, rest], axis=0)
    blank = jnp.zeros_like(record)
    both = jnp.concatenate(
        [jnp.concatenate([record, blank], 1), jnp.concatenate([blank, record], 1), jnp.zeros((64, 512), F32)], 0
    )
    spec_own[...] = dot_rows(basis_ref[...], both, precision=lax.Precision.HIGHEST)

    co_buf[1, q_me, :, 0:384] = coef_ref[...]
    co_buf[1, q_me, :, 384:768] = offs_ref[...].astype(F32)

    pl.semaphore_wait(barrier, SLAB - 1 + NX - 1)

    def send_spec(k, carry):
        y2 = lax.rem(y + lax.rem(k, NY), NY)
        zh2 = lax.rem(zh + lax.div(k, NY), NZH)
        block = (y2 * NZ + zh2 * NZL) // 4
        rows = pl.ds(pl.multiple_of(block * 8, 8), 8)
        remote(spec_own.at[rows], spec_buf.at[sen], spec_send, spec_recv, at(y2 * NZH + zh2, par))
        return carry

    lax.fori_loop(1, NY * NZH, send_spec, 0)

    for dq in range(1, 4):
        q2 = lax.rem(q_me + dq, 4)
        zl2, c2 = lax.div(q2, 2), lax.rem(q2, 2)
        remote(co_buf.at[1, q_me], co_buf.at[1, q_me], row_send, row_recv, at(sen, x * 4 + zl2 * 2 + c2))

    def send_op(k, carry):
        f2, dc, sen2, par2 = peer(k)
        remote(op_ref.at[:, f2], w_buf.at[c, zl, :, sen], op_send, op_recv.at[dc], at(sen2, par2))
        return carry

    lax.fori_loop(1, SLAB, send_op, 0)

    take(co_buf.at[1, pl.ds(0, 3)], row_recv)
    remote(co_buf.at[1], co_buf.at[0], co_send.at[0], co_recv.at[0], in_x(1))
    remote(co_buf.at[1], co_buf.at[2], co_send.at[1], co_recv.at[1], in_x(NX - 1))
    take(co_buf.at[0], co_recv.at[0])
    take(co_buf.at[2], co_recv.at[1])
    above, below = x > 0, x < NX - 1

    def rows_of(first):
        parts = []
        for b in range(3):
            for r in range(4):
                row = jnp.broadcast_to(co_buf[b, r, :, first : first + 384], (4, 384))
                if b == 0:
                    row = jnp.where(above, row, 0.0)
                if b == 2:
                    row = jnp.where(below, row, 0.0)
                parts.append(row)
        return jnp.concatenate(parts, axis=0)

    coef = rows_of(0)
    column = lax.broadcasted_iota(jnp.int32, (48, 384), 1)
    offs = rows_of(384).astype(jnp.int32)
    landed = column + offs
    offs = jnp.where((landed >= 0) & (landed < 384), offs, 99)

    def smooth(field):
        for _ in range(SWEEPS):
            upper = pltpu.roll(field, 4, 0)
            lower = pltpu.roll(field, 44, 0)
            linked = jnp.zeros_like(field)
            for shift in range(-3, 4):
                moved = lower if shift == 0 else pltpu.roll(lower, (-shift) % 384, 1)
                linked = jnp.where(offs == shift, moved, linked)
            left = jnp.where(column == 0, 0.0, pltpu.roll(field, 1, 1))
            right = jnp.where(column == 383, 0.0, pltpu.roll(field, 383, 1))
            field = field + coef * (left + right + upper + linked - 4.0 * field)
        return field

    take(spec_buf.at[pl.ds(0, NY * NZH - 1)], spec_recv)
    mine = pl.ds(pl.multiple_of(lax.div(f_me, 8) * 8, 8), 8)
    spec_buf[sen] = spec_own[mine, :]
    pick = lax.broadcasted_iota(jnp.int32, (32, 8, 128), 1) == lax.rem(f_me, 8)
    gathered = jnp.sum(jnp.where(pick, spec_buf[...], 0.0), axis=1)
    lane = lax.broadcasted_iota(jnp.int32, (32, 128), 1)
    sensor_row = lax.broadcasted_iota(jnp.int32, (32, 256), 0)
    sensor_lane = lax.broadcasted_iota(jnp.int32, (32, 256), 1) // 8
    whole = []
    for q in range(8):
        piece = jnp.where(lane // 8 == q, gathered, 0.0)
        for shift in (8, 16, 32, 64):
            piece = piece + pltpu.roll(piece, shift, 1)
        piece = jnp.concatenate([piece, piece], axis=1)
        whole.append(jnp.sum(jnp.where(sensor_row == sensor_lane, piece, 0.0), axis=0, keepdims=True))

    def stack(re, im):
        re, im = re.astype(BF16).astype(F32), im.astype(BF16).astype(F32)
        return jnp.concatenate(
            [jnp.concatenate([re, im], 1), jnp.concatenate([im, -re], 1)], 0
        ).astype(BF16)

    def weights(core, low):
        return w_buf[core, low].reshape(512, 384)

    def adjoint_of(h, spectra, core):
        for low in range(2):
            halo[h, 1, low * 2 + core] = jnp.dot(spectra, weights(core, low), preferred_element_type=F32)

    def rest_of(h):
        remote(halo.at[h, 1], halo.at[h, 0], halo_send.at[h, 0], halo_recv.at[h, 0], in_x(1))
        remote(halo.at[h, 1], halo.at[h, 2], halo_send.at[h, 1], halo_recv.at[h, 1], in_x(NX - 1))
        take(halo.at[h, 0], halo_recv.at[h, 0])
        take(halo.at[h, 2], halo_recv.at[h, 1])
        parts = []
        for b in range(3):
            for r in range(4):
                row = halo[h, b, r]
                if b == 0:
                    row = jnp.where(above, row, 0.0)
                if b == 2:
                    row = jnp.where(below, row, 0.0)
                parts.append(row)
        smoothed = smooth(jnp.concatenate(parts, axis=0))
        total = jnp.zeros((4, 512), F32)
        for q in range(4):
            prior = smoothed[16 + 4 * q : 20 + 4 * q].astype(BF16)
            total = total + dot_rows(prior, weights(q % 2, q // 2))
        sums[h, x] = jnp.concatenate(
            [total[0:2, :256] - total[2:4, 256:], total[2:4, :256] + total[0:2, 256:]], 0
        )
        for dx in range(1, NX):
            remote(sums.at[h, x], sums.at[h, x], sum_send.at[h], sum_recv.at[h], in_x(dx))
        take(sums.at[h, pl.ds(0, NX - 1)], sum_recv.at[h])
        forward = ((sums[h, 0] + sums[h, 1]) + sums[h, 2]) + sums[h, 3]
        rows = jnp.zeros((32, 128), F32)
        for q in range(4):
            piece = jnp.where(sensor_row == sensor_lane, jnp.broadcast_to(forward[q : q + 1], (32, 256)), 0.0)
            piece = piece[:, :128] + piece[:, 128:]
            for shift in (8, 16, 32, 64):
                piece = piece + pltpu.roll(piece, shift, 1)
            rows = jnp.where(lane // 8 == q, piece, rows)
        out_own[h] = rows.reshape(32, 1, 128)

        def send_out(k, carry):
            _, _, sen2, par2 = peer(k)
            remote(out_own.at[h, sen2], out_buf.at[h, f_me], out_send.at[h], out_recv.at[h], at(sen2, par2))
            return carry

        lax.fori_loop(1, SLAB, send_out, 0)
        out_buf[h, f_me] = out_own[h, sen]
        return forward

    def back_of(h):
        take(out_buf.at[h, pl.ds(0, SLAB - 1)], out_recv.at[h])
        got = out_buf[h].reshape(128, 128)
        dims = (((0,), (0,)), ((), ()))
        even = lax.dot_general(got, basis_ref[:, :256], dims, preferred_element_type=F32, precision=lax.Precision.HIGHEST)
        odd = lax.dot_general(got, basis_ref[:, 256:], dims, preferred_element_type=F32, precision=lax.Precision.HIGHEST)
        return even[0:16] + odd[16:32]

    first = stack(jnp.concatenate(whole[0:2], 0), jnp.concatenate(whole[4:6], 0))
    own_op.wait()
    take(op_ref.at[:, pl.ds(0, SLAB // 2 - 1)], op_recv.at[0])
    adjoint_of(0, first, c)
    take(op_ref.at[:, pl.ds(0, SLAB // 2)], op_recv.at[1])
    adjoint_of(0, first, 1 - c)
    forward = rest_of(0)
    second = stack(
        jnp.concatenate(whole[2:4], 0) - forward[0:2], jnp.concatenate(whole[6:8], 0) - forward[2:4]
    )
    adjoint_of(1, second, c)
    adjoint_of(1, second, 1 - c)
    rest_of(1)
    residual = rest - back_of(0)
    res_ref[...] = residual.reshape(2, 8, 256)
    app_ref[...] = (back_of(1) + noise16 * residual).reshape(2, 8, 256)

    take(op_ref.at[:, pl.ds(0, SLAB - 1)], op_send)
    take(spec_buf.at[pl.ds(0, NY * NZH - 1)], spec_send)
    take(co_buf.at[1, pl.ds(0, 3)], row_send)
    take(co_buf.at[0], co_send.at[0])
    take(co_buf.at[2], co_send.at[1])
    for h in range(2):
        take(halo.at[h, 0], halo_send.at[h, 0])
        take(halo.at[h, 2], halo_send.at[h, 1])
        take(sums.at[h, pl.ds(0, NX - 1)], sum_send.at[h])
        take(out_buf.at[h, pl.ds(0, SLAB - 1)], out_send.at[h])


def body(vectors, observed, operator, noise, coefficient, offsets):
    vmem = pl.BlockSpec(memory_space=pltpu.VMEM)
    dma = pltpu.SemaphoreType.DMA
    return pl.pallas_call(
        kernel,
        out_shape=(jax.ShapeDtypeStruct(vectors.shape, F32),) * 2,
        in_specs=[vmem, vmem, pl.BlockSpec(memory_space=pl.ANY), vmem, vmem, vmem, vmem],
        out_specs=(vmem, vmem),
        scratch_shapes=[
            pltpu.VMEM((2, 2, 2, 32, 8, 384), BF16),
            pltpu.VMEM((128, 128), F32),
            pltpu.VMEM((32, 8, 128), F32),
            pltpu.VMEM((3, 4, 1, 768), F32),
            pltpu.VMEM((2, 3, 4, 4, 384), F32),
            pltpu.VMEM((2, 4, 4, 256), F32),
            pltpu.VMEM((2, 32, 1, 128), F32),
            pltpu.VMEM((2, 128, 1, 128), F32),
            dma, dma((2,)), dma, dma, dma, dma, dma, dma((2,)), dma((2,)),
            dma((2, 2)), dma((2, 2)), dma((2,)), dma((2,)), dma((2,)), dma((2,)),
        ],
        compiler_params=pltpu.CompilerParams(
            collective_id=0, has_side_effects=True, vmem_limit_bytes=32 * 1024 * 1024
        ),
    )(vectors, observed, operator, noise.reshape(1, 8), coefficient, offsets, jnp.asarray(basis_rows(256)))


def solution(mesh):
    placed = (
        P(None, "sen", None),
        P(None, "sen", None),
        P(None, None, "sen", "par"),
        P("sen"),
        P("par", None),
        P("par", None),
    )
    return jax.shard_map(
        body,
        mesh=mesh,
        in_specs=placed,
        out_specs=(P(None, "sen", None), P(None, "sen", None)),
        check_vma=False,
    )
```

```python
import math

import jax
import jax.numpy as jnp
import numpy as np
from jax import lax
from jax.experimental import pallas as pl
from jax.experimental.pallas import tpu as pltpu
from jax.sharding import PartitionSpec as P

SWEEPS = 4
NY, NZH, NX, NZL = 8, 4, 4, 2
NZ = NZH * NZL
SLAB = NY * NZ * 2
STRIDE = 37
F32, BF16 = jnp.float32, jnp.bfloat16


def basis_rows(length):
    half = length // 2
    freqs = np.arange(half)[:, None]
    times = np.arange(length)[None, :]
    angle = ((2 * freqs + 1) * times % (2 * length)) * (math.pi / length)
    scale = math.sqrt(2.0 / length)
    return np.concatenate([np.cos(angle) * scale, np.sin(angle) * scale], 1).astype(np.float32)


def dot_rows(a, b, **kw):
    return lax.dot_general(a, b, (((1,), (1,)), ((), ())), preferred_element_type=F32, **kw)


def kernel(
    vec_hbm, obs_hbm, op_ref, noise_hbm, coef_hbm, offs_hbm, basis_hbm,
    res_ref, app_ref,
    vec_ref, obs_ref, noise_ref, coef_ref, offs_ref, basis_ref,
    w_buf, spec_own, spec_buf, co_buf, halo, sums, out_own, out_buf,
    load_sem, op_send, op_recv, op_local, spec_send, spec_recv, row_send, row_recv, co_send, co_recv,
    halo_send, halo_recv, sum_send, sum_recv, out_send, out_recv,
):
    sen = lax.axis_index("sen")
    par = lax.axis_index("par")
    x, q_me = lax.div(par, 4), lax.rem(par, 4)
    zl, c = lax.div(q_me, 2), lax.rem(q_me, 2)
    f_me = sen * 4 + q_me

    def peer(k):
        late = k // (SLAB // 2)
        f2 = lax.rem(f_me + STRIDE * (2 * k - (SLAB - 1) * late), SLAB)
        return f2, late, lax.div(f2, 4), par - q_me + lax.rem(f2, 4)

    def at(sen2, par2):
        return {"sen": sen2, "par": par2}

    def in_x(dx):
        return at(sen, lax.rem(x + dx, NX) * 4 + q_me)

    def remote(src, dst, send, recv, device):
        copy = pltpu.make_async_remote_copy(
            src_ref=src, dst_ref=dst, send_sem=send, recv_sem=recv,
            device_id=device, device_id_type=pl.DeviceIdType.MESH,
        )
        copy.start()

    def take(ref, sem):
        pltpu.make_async_copy(ref, ref, sem).wait()

    loads = []
    for i, (src, dst) in enumerate(
        ((vec_hbm, vec_ref), (obs_hbm, obs_ref), (noise_hbm, noise_ref),
         (coef_hbm, coef_ref), (offs_hbm, offs_ref), (basis_hbm, basis_ref))
    ):
        loads.append(pltpu.make_async_copy(src, dst, load_sem.at[i]))
        loads[-1].start()

    barrier = pltpu.get_barrier_semaphore()

    def greet(k, carry):
        _, _, sen2, par2 = peer(k)
        pl.semaphore_signal(barrier, inc=1, device_id=at(sen2, par2), device_id_type=pl.DeviceIdType.MESH)
        return carry

    lax.fori_loop(1, SLAB, greet, 0)
    for dx in range(1, NX):
        pl.semaphore_signal(barrier, inc=1, device_id=in_x(dx), device_id_type=pl.DeviceIdType.MESH)

    own_op = pltpu.make_async_copy(op_ref.at[:, f_me], w_buf.at[c, zl, :, sen], op_local)
    own_op.start()

    for load in loads:
        load.wait()
    eye = lax.broadcasted_iota(jnp.int32, (8, 8), 0) == lax.broadcasted_iota(jnp.int32, (8, 8), 1)
    noise = jnp.sum(jnp.where(eye, noise_ref[...], 0.0), axis=1, keepdims=True)
    noise16 = jnp.concatenate([noise, noise], axis=0)
    vec = vec_ref[...].reshape(16, 256)
    rest = obs_ref[...].reshape(16, 256) - noise16 * vec
    record = jnp.concatenate([vec, rest], axis=0)
    blank = jnp.zeros_like(record)
    both = jnp.concatenate(
        [jnp.concatenate([record, blank], 1), jnp.concatenate([blank, record], 1), jnp.zeros((64, 512), F32)], 0
    )
    spec_own[...] = dot_rows(basis_ref[...], both, precision=lax.Precision.HIGHEST)

    co_buf[1, q_me, :, 0:384] = coef_ref[...]
    co_buf[1, q_me, :, 384:768] = offs_ref[...].astype(F32)

    pl.semaphore_wait(barrier, SLAB - 1 + NX - 1)

    def send_spec(k, carry):
        sen2 = lax.rem(sen + 11 * k, NY * NZH)
        rows = pl.ds(pl.multiple_of(lax.div(sen2, 2) * 8, 8), 8)
        remote(spec_own.at[rows], spec_buf.at[sen], spec_send, spec_recv, at(sen2, par))
        return carry

    lax.fori_loop(1, NY * NZH, send_spec, 0)

    for dq in range(1, 4):
        q2 = lax.rem(q_me + dq, 4)
        zl2, c2 = lax.div(q2, 2), lax.rem(q2, 2)
        remote(co_buf.at[1, q_me], co_buf.at[1, q_me], row_send, row_recv, at(sen, x * 4 + zl2 * 2 + c2))

    def send_op(k, carry):
        f2, dc, sen2, par2 = peer(k)
        remote(op_ref.at[:, f2], w_buf.at[c, zl, :, sen], op_send, op_recv.at[dc], at(sen2, par2))
        return carry

    lax.fori_loop(1, SLAB, send_op, 0)

    take(co_buf.at[1, pl.ds(0, 3)], row_recv)
    remote(co_buf.at[1], co_buf.at[0], co_send.at[0], co_recv.at[0], in_x(1))
    remote(co_buf.at[1], co_buf.at[2], co_send.at[1], co_recv.at[1], in_x(NX - 1))
    take(co_buf.at[0], co_recv.at[0])
    take(co_buf.at[2], co_recv.at[1])
    above, below = x > 0, x < NX - 1

    def rows_of(first):
        parts = []
        for b in range(3):
            for r in range(4):
                row = jnp.broadcast_to(co_buf[b, r, :, first : first + 384], (4, 384))
                if b == 0:
                    row = jnp.where(above, row, 0.0)
                if b == 2:
                    row = jnp.where(below, row, 0.0)
                parts.append(row)
        return jnp.concatenate(parts, axis=0)

    coef = rows_of(0)
    column = lax.broadcasted_iota(jnp.int32, (48, 384), 1)
    offs = rows_of(384).astype(jnp.int32)
    landed = column + offs
    offs = jnp.where((landed >= 0) & (landed < 384), offs, 99)

    def smooth(field):
        for _ in range(SWEEPS):
            upper = pltpu.roll(field, 4, 0)
            lower = pltpu.roll(field, 44, 0)
            linked = jnp.zeros_like(field)
            for shift in range(-3, 4):
                moved = lower if shift == 0 else pltpu.roll(lower, (-shift) % 384, 1)
                linked = jnp.where(offs == shift, moved, linked)
            left = jnp.where(column == 0, 0.0, pltpu.roll(field, 1, 1))
            right = jnp.where(column == 383, 0.0, pltpu.roll(field, 383, 1))
            field = field + coef * (left + right + upper + linked - 4.0 * field)
        return field

    take(spec_buf.at[pl.ds(0, NY * NZH - 1)], spec_recv)
    mine = pl.ds(pl.multiple_of(lax.div(f_me, 8) * 8, 8), 8)
    spec_buf[sen] = spec_own[mine, :]
    pick = lax.broadcasted_iota(jnp.int32, (32, 8, 128), 1) == lax.rem(f_me, 8)
    gathered = jnp.sum(jnp.where(pick, spec_buf[...], 0.0), axis=1)
    lane = lax.broadcasted_iota(jnp.int32, (32, 128), 1)
    sensor_row = lax.broadcasted_iota(jnp.int32, (32, 256), 0)
    sensor_lane = lax.broadcasted_iota(jnp.int32, (32, 256), 1) // 8
    whole = []
    for q in range(8):
        piece = jnp.where(lane // 8 == q, gathered, 0.0)
        for shift in (8, 16, 32, 64):
            piece = piece + pltpu.roll(piece, shift, 1)
        piece = jnp.concatenate([piece, piece], axis=1)
        whole.append(jnp.sum(jnp.where(sensor_row == sensor_lane, piece, 0.0), axis=0, keepdims=True))

    def stack(re, im):
        re, im = re.astype(BF16).astype(F32), im.astype(BF16).astype(F32)
        return jnp.concatenate(
            [jnp.concatenate([re, im], 1), jnp.concatenate([im, -re], 1)], 0
        ).astype(BF16)

    def weights(core, low):
        return w_buf[core, low].reshape(512, 384)

    def adjoint_of(h, spectra, core):
        for low in range(2):
            halo[h, 1, low * 2 + core] = jnp.dot(spectra, weights(core, low), preferred_element_type=F32)

    def rest_of(h):
        remote(halo.at[h, 1], halo.at[h, 0], halo_send.at[h, 0], halo_recv.at[h, 0], in_x(1))
        remote(halo.at[h, 1], halo.at[h, 2], halo_send.at[h, 1], halo_recv.at[h, 1], in_x(NX - 1))
        take(halo.at[h, 0], halo_recv.at[h, 0])
        take(halo.at[h, 2], halo_recv.at[h, 1])
        parts = []
        for b in range(3):
            for r in range(4):
                row = halo[h, b, r]
                if b == 0:
                    row = jnp.where(above, row, 0.0)
                if b == 2:
                    row = jnp.where(below, row, 0.0)
                parts.append(row)
        smoothed = smooth(jnp.concatenate(parts, axis=0))
        total = jnp.zeros((4, 512), F32)
        for q in range(4):
            prior = smoothed[16 + 4 * q : 20 + 4 * q].astype(BF16)
            total = total + dot_rows(prior, weights(q % 2, q // 2))
        sums[h, x] = jnp.concatenate(
            [total[0:2, :256] - total[2:4, 256:], total[2:4, :256] + total[0:2, 256:]], 0
        )
        for dx in range(1, NX):
            remote(sums.at[h, x], sums.at[h, x], sum_send.at[h], sum_recv.at[h], in_x(dx))
        take(sums.at[h, pl.ds(0, NX - 1)], sum_recv.at[h])
        forward = ((sums[h, 0] + sums[h, 1]) + sums[h, 2]) + sums[h, 3]
        return forward

    def send_outs(forwards):
        rows = jnp.zeros((32, 128), F32)
        for q in range(8):
            row = forwards[q // 4][q % 4 : q % 4 + 1]
            piece = jnp.where(sensor_row == sensor_lane, jnp.broadcast_to(row, (32, 256)), 0.0)
            piece = piece[:, :128] + piece[:, 128:]
            for shift in (8, 16, 32, 64):
                piece = piece + pltpu.roll(piece, shift, 1)
            rows = jnp.where(lane // 8 == q, piece, rows)
        out_own[...] = rows.reshape(32, 1, 128)

        def send_out(k, carry):
            _, _, sen2, par2 = peer(k)
            remote(out_own.at[sen2], out_buf.at[f_me], out_send, out_recv, at(sen2, par2))
            return carry

        lax.fori_loop(1, SLAB, send_out, 0)
        out_buf[f_me] = out_own[sen]

    def backs():
        take(out_buf.at[pl.ds(0, SLAB - 1)], out_recv)
        got = out_buf[...].reshape(128, 128)
        dims = (((0,), (0,)), ((), ()))
        even = lax.dot_general(got, basis_ref[:, :256], dims, preferred_element_type=F32, precision=lax.Precision.HIGHEST)
        odd = lax.dot_general(got, basis_ref[:, 256:], dims, preferred_element_type=F32, precision=lax.Precision.HIGHEST)
        return even[0:16] + odd[16:32], even[32:48] + odd[48:64]

    first = stack(jnp.concatenate(whole[0:2], 0), jnp.concatenate(whole[4:6], 0))
    own_op.wait()
    take(op_ref.at[:, pl.ds(0, SLAB // 2 - 1)], op_recv.at[0])
    adjoint_of(0, first, c)
    take(op_ref.at[:, pl.ds(0, SLAB // 2)], op_recv.at[1])
    adjoint_of(0, first, 1 - c)
    forward = rest_of(0)
    second = stack(
        jnp.concatenate(whole[2:4], 0) - forward[0:2], jnp.concatenate(whole[6:8], 0) - forward[2:4]
    )
    adjoint_of(1, second, c)
    adjoint_of(1, second, 1 - c)
    send_outs((forward, rest_of(1)))
    back_0, back_1 = backs()
    residual = rest - back_0
    res_ref[...] = residual.reshape(2, 8, 256)
    app_ref[...] = (back_1 + noise16 * residual).reshape(2, 8, 256)

    take(op_ref.at[:, pl.ds(0, SLAB - 1)], op_send)
    take(spec_buf.at[pl.ds(0, NY * NZH - 1)], spec_send)
    take(co_buf.at[1, pl.ds(0, 3)], row_send)
    take(co_buf.at[0], co_send.at[0])
    take(co_buf.at[2], co_send.at[1])
    for h in range(2):
        take(halo.at[h, 0], halo_send.at[h, 0])
        take(halo.at[h, 2], halo_send.at[h, 1])
        take(sums.at[h, pl.ds(0, NX - 1)], sum_send.at[h])
    take(out_buf.at[pl.ds(0, SLAB - 1)], out_send)


def body(vectors, observed, operator, noise, coefficient, offsets):
    vmem = pl.BlockSpec(memory_space=pltpu.VMEM)
    dma = pltpu.SemaphoreType.DMA
    return pl.pallas_call(
        kernel,
        out_shape=(jax.ShapeDtypeStruct(vectors.shape, F32),) * 2,
        in_specs=[pl.BlockSpec(memory_space=pl.ANY)] * 7,
        out_specs=(vmem, vmem),
        scratch_shapes=[
            pltpu.VMEM((2, 8, 256), F32),
            pltpu.VMEM((2, 8, 256), F32),
            pltpu.VMEM((1, 8), F32),
            pltpu.VMEM((1, 384), F32),
            pltpu.VMEM((1, 384), jnp.int32),
            pltpu.VMEM((128, 512), F32),
            pltpu.VMEM((2, 2, 2, 32, 8, 384), BF16),
            pltpu.VMEM((128, 128), F32),
            pltpu.VMEM((32, 8, 128), F32),
            pltpu.VMEM((3, 4, 1, 768), F32),
            pltpu.VMEM((2, 3, 4, 4, 384), F32),
            pltpu.VMEM((2, 4, 4, 256), F32),
            pltpu.VMEM((32, 1, 128), F32),
            pltpu.VMEM((128, 1, 128), F32),
            dma((6,)), dma, dma((2,)), dma, dma, dma, dma, dma, dma((2,)), dma((2,)),
            dma((2, 2)), dma((2, 2)), dma((2,)), dma((2,)), dma, dma,
        ],
        compiler_params=pltpu.CompilerParams(
            collective_id=0, has_side_effects=True, vmem_limit_bytes=60 * 1024 * 1024
        ),
    )(vectors, observed, operator, noise.reshape(1, 8), coefficient, offsets, jnp.asarray(basis_rows(256)))


def solution(mesh):
    placed = (
        P(None, "sen", None),
        P(None, "sen", None),
        P(None, None, "sen", "par"),
        P("sen"),
        P("par", None),
        P("par", None),
    )
    return jax.shard_map(
        body,
        mesh=mesh,
        in_specs=placed,
        out_specs=(P(None, "sen", None), P(None, "sen", None)),
        check_vma=False,
    )
```

```python
import math

import jax
import jax.numpy as jnp
import numpy as np
from jax import lax
from jax.experimental import pallas as pl
from jax.experimental.pallas import tpu as pltpu
from jax.sharding import PartitionSpec as P

SWEEPS = 4
NY, NZH, NX, NZL = 8, 4, 4, 2
NZ = NZH * NZL
SLAB = NY * NZ * 2
STRIDE = 37
F32, BF16 = jnp.float32, jnp.bfloat16


def basis_rows(length):
    half = length // 2
    freqs = np.arange(half)[:, None]
    times = np.arange(length)[None, :]
    angle = ((2 * freqs + 1) * times % (2 * length)) * (math.pi / length)
    scale = math.sqrt(2.0 / length)
    return np.concatenate([np.cos(angle) * scale, np.sin(angle) * scale], 1).astype(np.float32)


def dot_rows(a, b, **kw):
    return lax.dot_general(a, b, (((1,), (1,)), ((), ())), preferred_element_type=F32, **kw)


def kernel(
    vec_hbm, obs_hbm, op_ref, noise_hbm, coef_hbm, offs_hbm, basis_hbm,
    res_ref, app_ref,
    vec_ref, obs_ref, noise_ref, coef_ref, offs_ref, basis_ref,
    w_buf, spec_own, spec_buf, co_buf, halo, sums, out_own, out_buf,
    load_sem, op_send, op_recv, op_local, spec_send, spec_recv, row_send, row_recv, co_send, co_recv,
    halo_send, halo_recv, sum_send, sum_recv, out_send, out_recv,
):
    sen = lax.axis_index("sen")
    par = lax.axis_index("par")
    x, q_me = lax.div(par, 4), lax.rem(par, 4)
    zl, c = lax.div(q_me, 2), lax.rem(q_me, 2)
    f_me = sen * 4 + q_me

    def wrap(value, size):
        return jnp.where(value >= size, value - size, value)

    def at(sen2, par2):
        return sen2 * (4 * NX) + par2

    def in_x(dx):
        return at(sen, wrap(x + dx, NX) * 4 + q_me)

    def each_block(act):
        def one(k, sen2):
            act(sen2)
            return wrap(sen2 + 11, NY * NZH)

        lax.fori_loop(1, NY * NZH, one, wrap(sen + 11, NY * NZH))

    def remote(src, dst, send, recv, device):
        copy = pltpu.make_async_remote_copy(
            src_ref=src, dst_ref=dst, send_sem=send, recv_sem=recv,
            device_id=device, device_id_type=pl.DeviceIdType.LOGICAL,
        )
        copy.start()

    def take(ref, sem):
        pltpu.make_async_copy(ref, ref, sem).wait()

    loads = []
    for i, (src, dst) in enumerate(
        ((vec_hbm, vec_ref), (obs_hbm, obs_ref), (noise_hbm, noise_ref),
         (coef_hbm, coef_ref), (offs_hbm, offs_ref), (basis_hbm, basis_ref))
    ):
        loads.append(pltpu.make_async_copy(src, dst, load_sem.at[i]))
        loads[-1].start()

    barrier = pltpu.get_barrier_semaphore()

    def tell(device):
        pl.semaphore_signal(barrier, inc=1, device_id=device, device_id_type=pl.DeviceIdType.LOGICAL)

    def greet(sen2):
        for q2 in range(4):
            tell(at(sen2, x * 4 + q2))

    each_block(greet)
    for dq in range(1, 4):
        tell(at(sen, x * 4 + wrap(q_me + dq, 4)))
    for dx in range(1, NX):
        tell(in_x(dx))

    own_op = pltpu.make_async_copy(op_ref.at[:, f_me], w_buf.at[c, zl, :, sen], op_local)
    own_op.start()

    for load in loads:
        load.wait()
    eye = lax.broadcasted_iota(jnp.int32, (8, 8), 0) == lax.broadcasted_iota(jnp.int32, (8, 8), 1)
    noise = jnp.sum(jnp.where(eye, noise_ref[...], 0.0), axis=1, keepdims=True)
    noise16 = jnp.concatenate([noise, noise], axis=0)
    vec = vec_ref[...].reshape(16, 256)
    rest = obs_ref[...].reshape(16, 256) - noise16 * vec
    record = jnp.concatenate([vec, rest], axis=0)
    blank = jnp.zeros_like(record)
    both = jnp.concatenate(
        [jnp.concatenate([record, blank], 1), jnp.concatenate([blank, record], 1), jnp.zeros((64, 512), F32)], 0
    )
    spec_own[...] = dot_rows(basis_ref[...], both, precision=lax.Precision.HIGHEST)

    co_buf[1, q_me, :, 0:384] = coef_ref[...]
    co_buf[1, q_me, :, 384:768] = offs_ref[...].astype(F32)

    pl.semaphore_wait(barrier, SLAB - 1 + NX - 1)

    def send_op(sen2, q2, core):
        remote(op_ref.at[:, sen2 * 4 + q2], w_buf.at[c, zl, :, sen], op_send, op_recv.at[core], at(sen2, x * 4 + q2))

    def send_core(core):
        mine = jnp.where(core == 0, c, 1 - c)

        def send_block(sen2):
            for low in range(2):
                send_op(sen2, low * 2 + mine, core)

        each_block(send_block)
        send_op(sen, (1 - zl) * 2 + mine, core)
        if core == 1:
            send_op(sen, zl * 2 + mine, core)

    send_core(0)

    def send_spec(sen2):
        rows = pl.ds(pl.multiple_of(lax.div(sen2, 2) * 8, 8), 8)
        remote(spec_own.at[rows], spec_buf.at[sen], spec_send, spec_recv, at(sen2, par))

    each_block(send_spec)
    for dq in range(1, 4):
        remote(
            co_buf.at[1, q_me], co_buf.at[1, q_me], row_send, row_recv, at(sen, x * 4 + wrap(q_me + dq, 4))
        )
    send_core(1)

    take(co_buf.at[1, pl.ds(0, 3)], row_recv)
    above, below = x > 0, x < NX - 1

    def to_neighbours(buf, send, recv):
        @pl.when(below)
        def _():
            remote(buf.at[1], buf.at[0], send.at[0], recv.at[0], par_at(x + 1))

        @pl.when(above)
        def _():
            remote(buf.at[1], buf.at[2], send.at[1], recv.at[1], par_at(x - 1))

    def from_neighbours(buf, recv):
        @pl.when(above)
        def _():
            take(buf.at[0], recv.at[0])

        @pl.when(below)
        def _():
            take(buf.at[2], recv.at[1])

    def par_at(x2):
        return at(sen, x2 * 4 + q_me)

    def clear(buf):
        @pl.when(x == 0)
        def _():
            buf[0] = jnp.zeros(buf.shape[1:], F32)

        @pl.when(x == NX - 1)
        def _():
            buf[2] = jnp.zeros(buf.shape[1:], F32)

    clear(co_buf)
    for h in range(2):
        clear(halo.at[h])
    to_neighbours(co_buf, co_send, co_recv)
    from_neighbours(co_buf, co_recv)

    def rows_of(first):
        parts = []
        for b in range(3):
            for r in range(4):
                parts.append(jnp.broadcast_to(co_buf[b, r, :, first : first + 384], (4, 384)))
        return jnp.concatenate(parts, axis=0)

    coef = rows_of(0)
    column = lax.broadcasted_iota(jnp.int32, (48, 384), 1)
    offs = rows_of(384).astype(jnp.int32)
    landed = column + offs
    offs = jnp.where((landed >= 0) & (landed < 384), offs, 99)

    def smooth(field):
        for _ in range(SWEEPS):
            upper = pltpu.roll(field, 4, 0)
            lower = pltpu.roll(field, 44, 0)
            linked = jnp.zeros_like(field)
            for shift in range(-3, 4):
                moved = lower if shift == 0 else pltpu.roll(lower, (-shift) % 384, 1)
                linked = jnp.where(offs == shift, moved, linked)
            left = jnp.where(column == 0, 0.0, pltpu.roll(field, 1, 1))
            right = jnp.where(column == 383, 0.0, pltpu.roll(field, 383, 1))
            field = field + coef * (left + right + upper + linked - 4.0 * field)
        return field

    take(spec_buf.at[pl.ds(0, NY * NZH - 1)], spec_recv)
    mine = pl.ds(pl.multiple_of(lax.div(f_me, 8) * 8, 8), 8)
    spec_buf[sen] = spec_own[mine, :]
    pick = lax.broadcasted_iota(jnp.int32, (32, 8, 128), 1) == lax.rem(f_me, 8)
    gathered = jnp.sum(jnp.where(pick, spec_buf[...], 0.0), axis=1)
    lane = lax.broadcasted_iota(jnp.int32, (32, 128), 1)
    sensor_row = lax.broadcasted_iota(jnp.int32, (32, 256), 0)
    sensor_lane = lax.broadcasted_iota(jnp.int32, (32, 256), 1) // 8
    whole = []
    for q in range(8):
        piece = jnp.where(lane // 8 == q, gathered, 0.0)
        for shift in (8, 16, 32, 64):
            piece = piece + pltpu.roll(piece, shift, 1)
        piece = jnp.concatenate([piece, piece], axis=1)
        whole.append(jnp.sum(jnp.where(sensor_row == sensor_lane, piece, 0.0), axis=0, keepdims=True))

    def stack(re, im):
        re, im = re.astype(BF16).astype(F32), im.astype(BF16).astype(F32)
        return jnp.concatenate(
            [jnp.concatenate([re, im], 1), jnp.concatenate([im, -re], 1)], 0
        ).astype(BF16)

    def weights(core, low):
        return w_buf[core, low].reshape(512, 384)

    def adjoint_of(h, spectra, core):
        for low in range(2):
            halo[h, 1, low * 2 + core] = jnp.dot(spectra, weights(core, low), preferred_element_type=F32)

    def rest_of(h, meanwhile):
        to_neighbours(halo.at[h], halo_send.at[h], halo_recv.at[h])
        done = meanwhile()
        from_neighbours(halo.at[h], halo_recv.at[h])
        parts = [halo[h, b, r] for b in range(3) for r in range(4)]
        smoothed = smooth(jnp.concatenate(parts, axis=0))
        total = jnp.zeros((4, 512), F32)
        for q in range(4):
            prior = smoothed[16 + 4 * q : 20 + 4 * q].astype(BF16)
            total = total + dot_rows(prior, weights(q % 2, q // 2))
        sums[h, x] = jnp.concatenate(
            [total[0:2, :256] - total[2:4, 256:], total[2:4, :256] + total[0:2, 256:]], 0
        )
        for dx in range(1, NX):
            remote(sums.at[h, x], sums.at[h, x], sum_send.at[h], sum_recv.at[h], in_x(dx))
        take(sums.at[h, pl.ds(0, NX - 1)], sum_recv.at[h])
        forward = ((sums[h, 0] + sums[h, 1]) + sums[h, 2]) + sums[h, 3]
        return forward, done

    def arrange(forward, rows, first):
        for q in range(4):
            piece = jnp.where(sensor_row == sensor_lane, jnp.broadcast_to(forward[q : q + 1], (32, 256)), 0.0)
            piece = piece[:, :128] + piece[:, 128:]
            for shift in (8, 16, 32, 64):
                piece = piece + pltpu.roll(piece, shift, 1)
            rows = jnp.where(lane // 8 == first + q, piece, rows)
        return rows

    def send_outs(rows):
        out_own[...] = rows.reshape(32, 1, 128)

        def send_out(sen2):
            for q2 in range(4):
                remote(out_own.at[sen2], out_buf.at[f_me], out_send, out_recv, at(sen2, x * 4 + q2))

        each_block(send_out)
        for dq in range(1, 4):
            remote(out_own.at[sen], out_buf.at[f_me], out_send, out_recv, at(sen, x * 4 + wrap(q_me + dq, 4)))
        out_buf[f_me] = out_own[sen]

    def backs():
        take(out_buf.at[pl.ds(0, SLAB - 1)], out_recv)
        got = out_buf[...].reshape(128, 128)
        dims = (((0,), (0,)), ((), ()))
        even = lax.dot_general(got, basis_ref[:, :256], dims, preferred_element_type=F32, precision=lax.Precision.HIGHEST)
        odd = lax.dot_general(got, basis_ref[:, 256:], dims, preferred_element_type=F32, precision=lax.Precision.HIGHEST)
        return even[0:16] + odd[16:32], even[32:48] + odd[48:64]

    first = stack(jnp.concatenate(whole[0:2], 0), jnp.concatenate(whole[4:6], 0))
    own_op.wait()
    take(op_ref.at[:, pl.ds(0, SLAB // 2 - 1)], op_recv.at[0])
    adjoint_of(0, first, c)
    take(op_ref.at[:, pl.ds(0, SLAB // 2)], op_recv.at[1])
    adjoint_of(0, first, 1 - c)
    forward, _ = rest_of(0, lambda: None)
    second = stack(
        jnp.concatenate(whole[2:4], 0) - forward[0:2], jnp.concatenate(whole[6:8], 0) - forward[2:4]
    )
    adjoint_of(1, second, c)
    adjoint_of(1, second, 1 - c)
    forward_1, rows = rest_of(1, lambda: arrange(forward, jnp.zeros((32, 128), F32), 0))
    send_outs(arrange(forward_1, rows, 4))
    back_0, back_1 = backs()
    residual = rest - back_0
    res_ref[...] = residual.reshape(2, 8, 256)
    app_ref[...] = (back_1 + noise16 * residual).reshape(2, 8, 256)

    take(op_ref.at[:, pl.ds(0, SLAB - 1)], op_send)
    take(spec_buf.at[pl.ds(0, NY * NZH - 1)], spec_send)
    take(co_buf.at[1, pl.ds(0, 3)], row_send)
    def sent(buf, send):
        @pl.when(below)
        def _():
            take(buf.at[0], send.at[0])

        @pl.when(above)
        def _():
            take(buf.at[2], send.at[1])

    sent(co_buf, co_send)
    for h in range(2):
        sent(halo.at[h], halo_send.at[h])
        take(sums.at[h, pl.ds(0, NX - 1)], sum_send.at[h])
    take(out_buf.at[pl.ds(0, SLAB - 1)], out_send)


def body(vectors, observed, operator, noise, coefficient, offsets):
    vmem = pl.BlockSpec(memory_space=pltpu.VMEM)
    dma = pltpu.SemaphoreType.DMA
    return pl.pallas_call(
        kernel,
        out_shape=(jax.ShapeDtypeStruct(vectors.shape, F32),) * 2,
        in_specs=[pl.BlockSpec(memory_space=pl.ANY)] * 7,
        out_specs=(vmem, vmem),
        scratch_shapes=[
            pltpu.VMEM((2, 8, 256), F32),
            pltpu.VMEM((2, 8, 256), F32),
            pltpu.VMEM((1, 8), F32),
            pltpu.VMEM((1, 384), F32),
            pltpu.VMEM((1, 384), jnp.int32),
            pltpu.VMEM((128, 512), F32),
            pltpu.VMEM((2, 2, 2, 32, 8, 384), BF16),
            pltpu.VMEM((128, 128), F32),
            pltpu.VMEM((32, 8, 128), F32),
            pltpu.VMEM((3, 4, 1, 768), F32),
            pltpu.VMEM((2, 3, 4, 4, 384), F32),
            pltpu.VMEM((2, 4, 4, 256), F32),
            pltpu.VMEM((32, 1, 128), F32),
            pltpu.VMEM((128, 1, 128), F32),
            dma((6,)), dma, dma((2,)), dma, dma, dma, dma, dma, dma((2,)), dma((2,)),
            dma((2, 2)), dma((2, 2)), dma((2,)), dma((2,)), dma, dma,
        ],
        compiler_params=pltpu.CompilerParams(
            collective_id=0, has_side_effects=True, vmem_limit_bytes=60 * 1024 * 1024
        ),
    )(vectors, observed, operator, noise.reshape(1, 8), coefficient, offsets, jnp.asarray(basis_rows(256)))


def solution(mesh):
    placed = (
        P(None, "sen", None),
        P(None, "sen", None),
        P(None, None, "sen", "par"),
        P("sen"),
        P("par", None),
        P("par", None),
    )
    return jax.shard_map(
        body,
        mesh=mesh,
        in_specs=placed,
        out_specs=(P(None, "sen", None), P(None, "sen", None)),
        check_vma=False,
    )
```

```python
import math

import jax
import jax.numpy as jnp
import numpy as np
from jax import lax
from jax.experimental import pallas as pl
from jax.experimental.pallas import tpu as pltpu
from jax.sharding import PartitionSpec as P

SWEEPS = 4
NY, NZH, NX, NZL = 8, 4, 4, 2
NZ = NZH * NZL
F32, BF16 = jnp.float32, jnp.bfloat16


def basis_rows(length):
    half = length // 2
    freqs = np.arange(half)[:, None]
    times = np.arange(length)[None, :]
    angle = ((2 * freqs + 1) * times % (2 * length)) * (math.pi / length)
    scale = math.sqrt(2.0 / length)
    return np.concatenate([np.cos(angle) * scale, np.sin(angle) * scale], 1).astype(np.float32)


def basis_split(rows):
    rest = np.concatenate(np.split(rows, 2, axis=1), 0)
    pieces = []
    for _ in range(3):
        pieces.append(rest.astype(BF16))
        rest = rest - pieces[-1].astype(np.float32)
    return np.stack(pieces)


def dot_rows(a, b, **kw):
    return lax.dot_general(a, b, (((1,), (1,)), ((), ())), preferred_element_type=F32, **kw)


def kernel(
    vec_hbm, obs_hbm, op_ref, noise_hbm, coef_hbm, offs_hbm, basis_hbm, split_hbm,
    res_ref, app_ref,
    vec_ref, obs_ref, noise_ref, coef_ref, offs_ref, basis_ref, split_ref,
    a_buf, b_buf, w_buf, spec_own, spec_row, spec_buf, co_buf, halo, sums, out_own, out_row, out_buf,
    load_sem, op_local, one_send, one_recv, two_send, two_recv,
    spec_send, spec_recv, spec_send_2, spec_recv_2, row_send, row_recv, co_send, co_recv,
    halo_send, halo_recv, sum_send, sum_recv, out_send, out_recv, out_send_2, out_recv_2,
):
    sen = lax.axis_index("sen")
    par = lax.axis_index("par")
    x, q_me = lax.div(par, 4), lax.rem(par, 4)
    zl, c = lax.div(q_me, 2), lax.rem(q_me, 2)

    def wrap(value, size):
        return jnp.where(value >= size, value - size, value)

    def at(sen2, par2):
        return sen2 * (4 * NX) + par2

    def in_x(dx):
        return at(sen, wrap(x + dx, NX) * 4 + q_me)

    y, zh = lax.div(sen, NZH), lax.rem(sen, NZH)
    zc = zh * 4 + q_me
    far_y = (4, 3, 5, 2, 6, 1, 7)
    far_z = [(dz, dq) for dz in (2, 1, 3, 0) for dq in range(4) if dz or dq]

    def dev(y2, zh2, q2):
        return at(y2 * NZH + zh2, x * 4 + q2)

    def in_y(dy):
        return wrap(y + dy, NY)

    def in_z(dz, dq):
        return wrap(zh + dz, NZH), wrap(q_me + dq, 4)

    def remote(src, dst, send, recv, device):
        copy = pltpu.make_async_remote_copy(
            src_ref=src, dst_ref=dst, send_sem=send, recv_sem=recv,
            device_id=device, device_id_type=pl.DeviceIdType.LOGICAL,
        )
        copy.start()

    def take(ref, sem):
        pltpu.make_async_copy(ref, ref, sem).wait()

    barrier = pltpu.get_barrier_semaphore()

    def tell(device):
        pl.semaphore_signal(barrier, inc=1, device_id=device, device_id_type=pl.DeviceIdType.LOGICAL)

    for dy in far_y:
        tell(dev(in_y(dy), zh, q_me))
    for dz, dq in far_z:
        tell(dev(y, *in_z(dz, dq)))
    for dx in range(1, NX):
        tell(in_x(dx))

    loads = []
    for i, (src, dst) in enumerate(
        ((vec_hbm, vec_ref), (obs_hbm, obs_ref), (noise_hbm, noise_ref),
         (coef_hbm, coef_ref), (offs_hbm, offs_ref), (basis_hbm, basis_ref), (split_hbm, split_ref))
    ):
        loads.append(pltpu.make_async_copy(src, dst, load_sem.at[i]))
        loads[-1].start()

    own = [
        pltpu.make_async_copy(op_ref.at[0, y], a_buf.at[y], op_local.at[0]),
        pltpu.make_async_copy(op_ref.at[1, :, zc], b_buf.at[c, zl, zh], op_local.at[1]),
    ]
    for copy in own:
        copy.start()

    pl.semaphore_wait(barrier, 22 + NX - 1)

    half_y, half_z = lax.div(y, 4), lax.div(zh, 2)

    def first_stage(sub):
        to_y = 1 - half_y if sub == 0 else half_y
        to_z = 1 - half_z if sub == 0 else half_z
        cut_y = pl.ds(to_y * 4, 4)
        cut_z = pl.ds(to_z * 8, 8)
        for n, (dz, dq) in enumerate(far_z):
            if n % 2 == 0 and n // 2 < 7:
                y2 = in_y(far_y[n // 2])
                remote(
                    op_ref.at[0, y2, cut_z], a_buf.at[y, cut_z],
                    one_send.at[0], one_recv.at[0, sub], dev(y2, zh, q_me),
                )
            zh2, q2 = in_z(dz, dq)
            remote(
                op_ref.at[1, cut_y, zh2 * 4 + q2], b_buf.at[c, zl, zh, cut_y],
                one_send.at[1], one_recv.at[1, sub], dev(y, zh2, q2),
            )

    first_stage(0)

    for load in loads[:6]:
        load.wait()
    eye = lax.broadcasted_iota(jnp.int32, (8, 8), 0) == lax.broadcasted_iota(jnp.int32, (8, 8), 1)
    noise = jnp.sum(jnp.where(eye, noise_ref[...], 0.0), axis=1, keepdims=True)
    noise16 = jnp.concatenate([noise, noise], axis=0)
    vec = vec_ref[...].reshape(16, 256)
    rest = obs_ref[...].reshape(16, 256) - noise16 * vec
    record = jnp.concatenate([vec, rest], axis=0)
    blank = jnp.zeros_like(record)
    both = jnp.concatenate(
        [jnp.concatenate([record, blank], 1), jnp.concatenate([blank, record], 1), jnp.zeros((64, 512), F32)], 0
    )
    spec_own[...] = dot_rows(basis_ref[...], both, precision=lax.Precision.HIGHEST)

    co_buf[1, q_me, :, 0:384] = coef_ref[...]
    co_buf[1, q_me, :, 384:768] = offs_ref[...].astype(F32)

    for dy in far_y:
        y2 = in_y(dy)
        rows = pl.ds(pl.multiple_of(y2 * 16, 16), 16)
        remote(spec_own.at[rows], spec_row.at[y], spec_send, spec_recv, dev(y2, zh, q_me))
    for dq in range(1, 4):
        remote(co_buf.at[1, q_me], co_buf.at[1, q_me], row_send, row_recv, dev(y, zh, wrap(q_me + dq, 4)))

    first_stage(1)

    take(co_buf.at[1, pl.ds(0, 3)], row_recv)
    above, below = x > 0, x < NX - 1

    def to_neighbours(buf, send, recv):
        @pl.when(below)
        def _():
            remote(buf.at[1], buf.at[0], send.at[0], recv.at[0], par_at(x + 1))

        @pl.when(above)
        def _():
            remote(buf.at[1], buf.at[2], send.at[1], recv.at[1], par_at(x - 1))

    def from_neighbours(buf, recv):
        @pl.when(above)
        def _():
            take(buf.at[0], recv.at[0])

        @pl.when(below)
        def _():
            take(buf.at[2], recv.at[1])

    def par_at(x2):
        return at(sen, x2 * 4 + q_me)

    def clear(buf):
        @pl.when(x == 0)
        def _():
            buf[0] = jnp.zeros(buf.shape[1:], F32)

        @pl.when(x == NX - 1)
        def _():
            buf[2] = jnp.zeros(buf.shape[1:], F32)

    clear(co_buf)
    for h in range(2):
        clear(halo.at[h])
    to_neighbours(co_buf, co_send, co_recv)

    take(spec_row.at[pl.ds(0, NY - 1)], spec_recv)
    spec_row[y] = spec_own[pl.ds(pl.multiple_of(y * 16, 16), 16), :]
    for dz in range(1, NZH):
        zh2 = wrap(zh + dz, NZH)
        rows = pl.ds(pl.multiple_of(lax.div(zh2, 2) * 8, 8), 8)
        remote(spec_row.at[:, rows], spec_buf.at[:, zh], spec_send_2, spec_recv_2, dev(y, zh2, q_me))

    def send_z(zh2, q2):
        remote(
            a_buf.at[:, zh2 * 4 + q2], w_buf.at[c, zl, 0, :, zh], two_send.at[0], two_recv.at[0], dev(y, zh2, q2)
        )

    def send_y(y2):
        remote(b_buf.at[:, :, :, y2], w_buf.at[:, :, 1, y], two_send.at[1], two_recv.at[1], dev(y2, zh, q_me))

    half_a = op_ref.at[0, pl.ds(0, NY - 1), pl.ds(0, 8)]
    half_b = op_ref.at[0, pl.ds(0, 4), pl.ds(0, 15)]
    whole_a = op_ref.at[0, pl.ds(0, NY - 1)]
    whole_b = op_ref.at[0, :, pl.ds(0, 15)]
    for copy in own:
        copy.wait()
    take(half_a, one_recv.at[0, 0])
    for low in range(2):
        for q2 in range(4):
            send_z((1 - half_z) * 2 + low, q2)
    take(half_b, one_recv.at[1, 0])
    for low in range(4):
        send_y((1 - half_y) * 4 + low)
    take(half_a, one_recv.at[0, 1])
    for q2 in range(4):
        send_z(half_z * 4 + 1 - zh, q2)
    for dq in range(1, 4):
        send_z(zh, wrap(q_me + dq, 4))
    take(half_b, one_recv.at[1, 1])
    for dy in range(1, 4):
        send_y(half_y * 4 + wrap(y - half_y * 4 + dy, 4))
    kept = [
        pltpu.make_async_copy(a_buf.at[:, zc], w_buf.at[c, zl, 0, :, zh], op_local.at[0]),
        pltpu.make_async_copy(b_buf.at[:, :, :, y], w_buf.at[:, :, 1, y], op_local.at[1]),
    ]
    for copy in kept:
        copy.start()

    from_neighbours(co_buf, co_recv)

    def rows_of(first):
        parts = []
        for b in range(3):
            for r in range(4):
                parts.append(jnp.broadcast_to(co_buf[b, r, :, first : first + 384], (4, 384)))
        return jnp.concatenate(parts, axis=0)

    coef = rows_of(0)
    column = lax.broadcasted_iota(jnp.int32, (48, 384), 1)
    offs = rows_of(384).astype(jnp.int32)
    landed = column + offs
    offs = jnp.where((landed >= 0) & (landed < 384), offs, 99)

    def sweep(field, top, low, high):
        here = slice(low - top, high - top)
        u = field[here]
        rows = field.shape[0]
        upper = pltpu.roll(field, 4, 0)[here]
        lower = pltpu.roll(field, rows - 4, 0)[here]
        near_off, across = offs[low:high], column[low:high]
        linked = jnp.zeros_like(u)
        for shift in range(-3, 4):
            moved = lower if shift == 0 else pltpu.roll(lower, (-shift) % 384, 1)
            linked = jnp.where(near_off == shift, moved, linked)
        left = jnp.where(across == 0, 0.0, pltpu.roll(u, 1, 1))
        right = jnp.where(across == 383, 0.0, pltpu.roll(u, 383, 1))
        return u + coef[low:high] * (left + right + upper + linked - 4.0 * u)

    def smooth(field):
        field = sweep(field, 0, 0, 48)
        field = sweep(field, 0, 8, 40)
        field = sweep(field, 8, 8, 40)
        return sweep(field, 8, 16, 32)

    take(spec_buf.at[:, pl.ds(0, NZH - 1)], spec_recv_2)
    mine = pl.ds(pl.multiple_of(lax.div(zc, 8) * 8, 8), 8)
    spec_buf[:, zh] = spec_row[:, mine, :]
    pick = lax.broadcasted_iota(jnp.int32, (32, 8, 128), 1) == lax.rem(zc, 8)
    gathered = jnp.sum(jnp.where(pick, spec_buf[...].reshape(32, 8, 128), 0.0), axis=1)
    lane = lax.broadcasted_iota(jnp.int32, (32, 128), 1)
    sensor_row = lax.broadcasted_iota(jnp.int32, (32, 256), 0)
    sensor_lane = lax.broadcasted_iota(jnp.int32, (32, 256), 1) // 8
    whole = []
    for q in range(8):
        piece = jnp.where(lane // 8 == q, gathered, 0.0)
        for shift in (8, 16, 32, 64):
            piece = piece + pltpu.roll(piece, shift, 1)
        piece = jnp.concatenate([piece, piece], axis=1)
        whole.append(jnp.sum(jnp.where(sensor_row == sensor_lane, piece, 0.0), axis=0, keepdims=True))

    def stack(re, im):
        re, im = re.astype(BF16).astype(F32), im.astype(BF16).astype(F32)
        return jnp.concatenate(
            [jnp.concatenate([re, im], 1), jnp.concatenate([im, -re], 1)], 0
        ).astype(BF16)

    def weights(core, low):
        return w_buf[core, low].reshape(512, 384)

    def adjoint_of(h, spectra):
        for q in range(4):
            halo[h, 1, q] = jnp.dot(spectra, weights(q % 2, q // 2), preferred_element_type=F32)

    def rest_of(h, meanwhile):
        to_neighbours(halo.at[h], halo_send.at[h], halo_recv.at[h])
        done = meanwhile()
        from_neighbours(halo.at[h], halo_recv.at[h])
        parts = [halo[h, b, r] for b in range(3) for r in range(4)]
        smoothed = smooth(jnp.concatenate(parts, axis=0))
        total = jnp.zeros((4, 512), F32)
        for q in range(4):
            prior = smoothed[4 * q : 4 * q + 4].astype(BF16)
            total = total + dot_rows(prior, weights(q % 2, q // 2))
        sums[h, x] = jnp.concatenate(
            [total[0:2, :256] - total[2:4, 256:], total[2:4, :256] + total[0:2, 256:]], 0
        )
        for dx in range(1, NX):
            remote(sums.at[h, x], sums.at[h, x], sum_send.at[h], sum_recv.at[h], in_x(dx))
        take(sums.at[h, pl.ds(0, NX - 1)], sum_recv.at[h])
        forward = ((sums[h, 0] + sums[h, 1]) + sums[h, 2]) + sums[h, 3]
        return forward, done

    def arrange(forward, rows, first):
        for q in range(4):
            piece = jnp.where(sensor_row == sensor_lane, jnp.broadcast_to(forward[q : q + 1], (32, 256)), 0.0)
            piece = piece[:, :128] + piece[:, 128:]
            for shift in (8, 16, 32, 64):
                piece = piece + pltpu.roll(piece, shift, 1)
            rows = jnp.where(lane // 8 == (q // 2) * 4 + first + q % 2, piece, rows)
        return rows

    def send_outs(rows):
        out_own[...] = rows.reshape(NY, NZH, 1, 128)

        for dy in far_y:
            y2 = in_y(dy)
            remote(out_own.at[y2], out_row.at[y], out_send, out_recv, dev(y2, zh, q_me))
        out_row[y] = out_own[y]
        take(out_row.at[pl.ds(0, NY - 1)], out_recv)
        for dz, dq in far_z:
            zh2, q2 = in_z(dz, dq)
            remote(out_row.at[:, zh2], out_buf.at[:, zc], out_send_2, out_recv_2, dev(y, zh2, q2))
        out_buf[:, zc] = out_row[:, zh]

    def backs():
        take(out_buf.at[:, pl.ds(0, 15)], out_recv_2)
        loads[6].wait()
        got = out_buf[...].reshape(128, 128)
        left = jnp.concatenate([got[:, :32], got[:, 32:64]], 0).T
        pieces = []
        for _ in range(3):
            pieces.append(left.astype(BF16))
            left = left - pieces[-1].astype(F32)
        total = jnp.zeros((32, 256), F32)
        for a, b in ((2, 0), (0, 2), (1, 1), (1, 0), (0, 1), (0, 0)):
            total = total + jnp.dot(pieces[a], split_ref[b], preferred_element_type=F32)
        return total[:16], total[16:]

    first = stack(jnp.concatenate(whole[0:2], 0), jnp.concatenate(whole[4:6], 0))
    for copy in kept:
        copy.wait()
    take(whole_b, two_recv.at[0])
    take(whole_a, two_recv.at[1])
    adjoint_of(0, first)
    forward, _ = rest_of(0, lambda: None)
    second = stack(
        jnp.concatenate(whole[2:4], 0) - forward[0:2], jnp.concatenate(whole[6:8], 0) - forward[2:4]
    )
    adjoint_of(1, second)
    forward_1, rows = rest_of(1, lambda: arrange(forward, jnp.zeros((32, 128), F32), 0))
    send_outs(arrange(forward_1, rows, 2))
    back_0, back_1 = backs()
    residual = rest - back_0
    res_ref[...] = residual.reshape(2, 8, 256)
    app_ref[...] = (back_1 + noise16 * residual).reshape(2, 8, 256)

    take(whole_a, one_send.at[0])
    take(whole_b, one_send.at[1])
    take(whole_b, two_send.at[0])
    take(whole_a, two_send.at[1])
    take(spec_row.at[pl.ds(0, NY - 1)], spec_send)
    take(spec_buf.at[:, pl.ds(0, NZH - 1)], spec_send_2)
    take(co_buf.at[1, pl.ds(0, 3)], row_send)
    def sent(buf, send):
        @pl.when(below)
        def _():
            take(buf.at[0], send.at[0])

        @pl.when(above)
        def _():
            take(buf.at[2], send.at[1])

    sent(co_buf, co_send)
    for h in range(2):
        sent(halo.at[h], halo_send.at[h])
        take(sums.at[h, pl.ds(0, NX - 1)], sum_send.at[h])
    take(out_row.at[pl.ds(0, NY - 1)], out_send)
    take(out_buf.at[:, pl.ds(0, 15)], out_send_2)


def body(vectors, observed, operator, noise, coefficient, offsets):
    rows = basis_rows(vectors.shape[-1])
    vmem = pl.BlockSpec(memory_space=pltpu.VMEM)
    dma = pltpu.SemaphoreType.DMA
    return pl.pallas_call(
        kernel,
        out_shape=(jax.ShapeDtypeStruct(vectors.shape, F32),) * 2,
        in_specs=[pl.BlockSpec(memory_space=pl.ANY)] * 8,
        out_specs=(vmem, vmem),
        scratch_shapes=[
            pltpu.VMEM((2, 8, 256), F32),
            pltpu.VMEM((2, 8, 256), F32),
            pltpu.VMEM((1, 8), F32),
            pltpu.VMEM((1, 384), F32),
            pltpu.VMEM((1, 384), jnp.int32),
            pltpu.VMEM((128, 512), F32),
            pltpu.VMEM((3, 256, 256), BF16),
            pltpu.VMEM((NY, 16, 8, 384), BF16),
            pltpu.VMEM((2, 2, NZH, NY, 8, 384), BF16),
            pltpu.VMEM((2, 2, 2, NY, NZH, 8, 384), BF16),
            pltpu.VMEM((128, 128), F32),
            pltpu.VMEM((NY, 16, 128), F32),
            pltpu.VMEM((NY, NZH, 8, 128), F32),
            pltpu.VMEM((3, 4, 1, 768), F32),
            pltpu.VMEM((2, 3, 4, 4, 384), F32),
            pltpu.VMEM((2, 4, 4, 256), F32),
            pltpu.VMEM((NY, NZH, 1, 128), F32),
            pltpu.VMEM((NY, NZH, 1, 128), F32),
            pltpu.VMEM((NY, 16, 1, 128), F32),
            dma((7,)), dma((2,)), dma((2,)), dma((2, 2)), dma((2,)), dma((2,)),
            dma, dma, dma, dma, dma, dma, dma((2,)), dma((2,)),
            dma((2, 2)), dma((2, 2)), dma((2,)), dma((2,)), dma, dma, dma, dma,
        ],
        compiler_params=pltpu.CompilerParams(
            collective_id=0, has_side_effects=True, vmem_limit_bytes=60 * 1024 * 1024
        ),
    )(vectors, observed, operator.reshape(2, NY, 16, 8, 384), noise.reshape(1, 8), coefficient, offsets, jnp.asarray(rows), jnp.asarray(basis_split(rows)))


def solution(mesh):
    placed = (
        P(None, "sen", None),
        P(None, "sen", None),
        P(None, None, "sen", "par"),
        P("sen"),
        P("par", None),
        P("par", None),
    )
    return jax.shard_map(
        body,
        mesh=mesh,
        in_specs=placed,
        out_specs=(P(None, "sen", None), P(None, "sen", None)),
        check_vma=False,
    )
```

```python
import math

import jax
import jax.numpy as jnp
import numpy as np
from jax import lax
from jax.experimental import pallas as pl
from jax.experimental.pallas import tpu as pltpu
from jax.sharding import PartitionSpec as P

SWEEPS = 4
NY, NZH, NX, NZL = 8, 4, 4, 2
NZ = NZH * NZL
F32, BF16 = jnp.float32, jnp.bfloat16


def basis_rows(length):
    half = length // 2
    freqs = np.arange(half)[:, None]
    times = np.arange(length)[None, :]
    angle = ((2 * freqs + 1) * times % (2 * length)) * (math.pi / length)
    scale = math.sqrt(2.0 / length)
    return np.concatenate([np.cos(angle) * scale, np.sin(angle) * scale], 1).astype(np.float32)


def basis_split(rows):
    rest = np.concatenate(np.split(rows, 2, axis=1), 0)
    pieces = []
    for _ in range(3):
        pieces.append(rest.astype(BF16))
        rest = rest - pieces[-1].astype(np.float32)
    return np.stack(pieces)


def dot_rows(a, b, **kw):
    return lax.dot_general(a, b, (((1,), (1,)), ((), ())), preferred_element_type=F32, **kw)


def kernel(
    vec_hbm, obs_hbm, op_ref, noise_hbm, coef_hbm, offs_hbm, basis_hbm, split_hbm,
    res_ref, app_ref,
    vec_ref, obs_ref, noise_ref, coef_ref, offs_ref, basis_ref, split_ref,
    a_buf, b_buf, w_buf, spec_own, spec_row, spec_buf, co_buf, halo, sums, out_own, out_buf,
    load_sem, op_local, one_send, one_recv, two_send, two_recv,
    spec_send, spec_recv, spec_send_2, spec_recv_2, row_send, row_recv, co_send, co_recv,
    halo_send, halo_recv, sum_send, sum_recv, out_send, out_recv,
):
    sen = lax.axis_index("sen")
    par = lax.axis_index("par")
    x, q_me = lax.div(par, 4), lax.rem(par, 4)
    zl, c = lax.div(q_me, 2), lax.rem(q_me, 2)

    def wrap(value, size):
        return jnp.where(value >= size, value - size, value)

    def at(sen2, par2):
        return sen2 * (4 * NX) + par2

    def in_x(dx):
        return at(sen, wrap(x + dx, NX) * 4 + q_me)

    y, zh = lax.div(sen, NZH), lax.rem(sen, NZH)
    zc = zh * 4 + q_me
    far_y = (4, 3, 5, 2, 6, 1, 7)
    far_z = [(dz, dq) for dz in (2, 1, 3, 0) for dq in range(4) if dz or dq]

    def dev(y2, zh2, q2):
        return at(y2 * NZH + zh2, x * 4 + q2)

    def in_y(dy):
        return wrap(y + dy, NY)

    def in_z(dz, dq):
        return wrap(zh + dz, NZH), wrap(q_me + dq, 4)

    def remote(src, dst, send, recv, device):
        copy = pltpu.make_async_remote_copy(
            src_ref=src, dst_ref=dst, send_sem=send, recv_sem=recv,
            device_id=device, device_id_type=pl.DeviceIdType.LOGICAL,
        )
        copy.start()

    def take(ref, sem):
        pltpu.make_async_copy(ref, ref, sem).wait()

    barrier = pltpu.get_barrier_semaphore()

    def tell(device):
        pl.semaphore_signal(barrier, inc=1, device_id=device, device_id_type=pl.DeviceIdType.LOGICAL)

    for dy in far_y:
        tell(dev(in_y(dy), zh, q_me))
    for dz, dq in far_z:
        tell(dev(y, *in_z(dz, dq)))
    for dx in range(1, NX):
        tell(in_x(dx))

    loads = []
    for i, (src, dst) in enumerate(
        ((vec_hbm, vec_ref), (obs_hbm, obs_ref), (noise_hbm, noise_ref),
         (coef_hbm, coef_ref), (offs_hbm, offs_ref), (basis_hbm, basis_ref), (split_hbm, split_ref))
    ):
        loads.append(pltpu.make_async_copy(src, dst, load_sem.at[i]))
        loads[-1].start()

    own = [
        pltpu.make_async_copy(op_ref.at[0, y], a_buf.at[y], op_local.at[0]),
        pltpu.make_async_copy(op_ref.at[1, :, zc], b_buf.at[c, zl, zh], op_local.at[1]),
    ]
    for copy in own:
        copy.start()

    pl.semaphore_wait(barrier, 22 + NX - 1)

    half_y, half_z = lax.div(y, 4), lax.div(zh, 2)

    def first_stage(sub):
        to_y = 1 - half_y if sub == 0 else half_y
        to_z = 1 - half_z if sub == 0 else half_z
        cut_y = pl.ds(to_y * 4, 4)
        cut_z = pl.ds(to_z * 8, 8)
        for n, (dz, dq) in enumerate(far_z):
            if n % 2 == 0 and n // 2 < 7:
                y2 = in_y(far_y[n // 2])
                remote(
                    op_ref.at[0, y2, cut_z], a_buf.at[y, cut_z],
                    one_send.at[0], one_recv.at[0, sub], dev(y2, zh, q_me),
                )
            zh2, q2 = in_z(dz, dq)
            remote(
                op_ref.at[1, cut_y, zh2 * 4 + q2], b_buf.at[c, zl, zh, cut_y],
                one_send.at[1], one_recv.at[1, sub], dev(y, zh2, q2),
            )

    first_stage(0)

    for load in loads[:6]:
        load.wait()
    eye = lax.broadcasted_iota(jnp.int32, (8, 8), 0) == lax.broadcasted_iota(jnp.int32, (8, 8), 1)
    noise = jnp.sum(jnp.where(eye, noise_ref[...], 0.0), axis=1, keepdims=True)
    noise16 = jnp.concatenate([noise, noise], axis=0)
    vec = vec_ref[...].reshape(16, 256)
    rest = obs_ref[...].reshape(16, 256) - noise16 * vec
    record = jnp.concatenate([vec, rest], axis=0)
    blank = jnp.zeros_like(record)
    both = jnp.concatenate(
        [jnp.concatenate([record, blank], 1), jnp.concatenate([blank, record], 1), jnp.zeros((64, 512), F32)], 0
    )
    spec_own[...] = dot_rows(basis_ref[...], both, precision=lax.Precision.HIGHEST)

    co_buf[1, q_me, :, 0:384] = coef_ref[...]
    co_buf[1, q_me, :, 384:768] = offs_ref[...].astype(F32)

    for dy in far_y:
        y2 = in_y(dy)
        rows = pl.ds(pl.multiple_of(y2 * 16, 16), 16)
        remote(spec_own.at[rows], spec_row.at[y], spec_send, spec_recv, dev(y2, zh, q_me))
    for dq in range(1, 4):
        remote(co_buf.at[1, q_me], co_buf.at[1, q_me], row_send, row_recv, dev(y, zh, wrap(q_me + dq, 4)))

    first_stage(1)

    take(co_buf.at[1, pl.ds(0, 3)], row_recv)
    above, below = x > 0, x < NX - 1

    def to_neighbours(buf, send, recv):
        @pl.when(below)
        def _():
            remote(buf.at[1], buf.at[0], send.at[0], recv.at[0], par_at(x + 1))

        @pl.when(above)
        def _():
            remote(buf.at[1], buf.at[2], send.at[1], recv.at[1], par_at(x - 1))

    def from_neighbours(buf, recv):
        @pl.when(above)
        def _():
            take(buf.at[0], recv.at[0])

        @pl.when(below)
        def _():
            take(buf.at[2], recv.at[1])

    def par_at(x2):
        return at(sen, x2 * 4 + q_me)

    def clear(buf):
        @pl.when(x == 0)
        def _():
            buf[0] = jnp.zeros(buf.shape[1:], F32)

        @pl.when(x == NX - 1)
        def _():
            buf[2] = jnp.zeros(buf.shape[1:], F32)

    clear(co_buf)
    for h in range(2):
        clear(halo.at[h])
    to_neighbours(co_buf, co_send, co_recv)

    take(spec_row.at[pl.ds(0, NY - 1)], spec_recv)
    spec_row[y] = spec_own[pl.ds(pl.multiple_of(y * 16, 16), 16), :]
    for dz in range(1, NZH):
        zh2 = wrap(zh + dz, NZH)
        rows = pl.ds(pl.multiple_of(lax.div(zh2, 2) * 8, 8), 8)
        remote(spec_row.at[:, rows], spec_buf.at[:, zh], spec_send_2, spec_recv_2, dev(y, zh2, q_me))

    def send_z(zh2, q2):
        remote(
            a_buf.at[:, zh2 * 4 + q2], w_buf.at[c, zl, 0, :, zh], two_send.at[0], two_recv.at[0], dev(y, zh2, q2)
        )

    def send_y(y2):
        remote(b_buf.at[:, :, :, y2], w_buf.at[:, :, 1, y], two_send.at[1], two_recv.at[1], dev(y2, zh, q_me))

    half_a = op_ref.at[0, pl.ds(0, NY - 1), pl.ds(0, 8)]
    half_b = op_ref.at[0, pl.ds(0, 4), pl.ds(0, 15)]
    whole_a = op_ref.at[0, pl.ds(0, NY - 1)]
    whole_b = op_ref.at[0, :, pl.ds(0, 15)]
    for copy in own:
        copy.wait()
    take(half_a, one_recv.at[0, 0])
    for low in range(2):
        for q2 in range(4):
            send_z((1 - half_z) * 2 + low, q2)
    take(half_b, one_recv.at[1, 0])
    for low in range(4):
        send_y((1 - half_y) * 4 + low)
    take(half_a, one_recv.at[0, 1])
    for q2 in range(4):
        send_z(half_z * 4 + 1 - zh, q2)
    for dq in range(1, 4):
        send_z(zh, wrap(q_me + dq, 4))
    take(half_b, one_recv.at[1, 1])
    for dy in range(1, 4):
        send_y(half_y * 4 + wrap(y - half_y * 4 + dy, 4))
    kept = [
        pltpu.make_async_copy(a_buf.at[:, zc], w_buf.at[c, zl, 0, :, zh], op_local.at[0]),
        pltpu.make_async_copy(b_buf.at[:, :, :, y], w_buf.at[:, :, 1, y], op_local.at[1]),
    ]
    for copy in kept:
        copy.start()

    from_neighbours(co_buf, co_recv)

    def rows_of(first):
        parts = []
        for b in range(3):
            for r in range(4):
                parts.append(jnp.broadcast_to(co_buf[b, r, :, first : first + 384], (4, 384)))
        return jnp.concatenate(parts, axis=0)

    coef = rows_of(0)
    column = lax.broadcasted_iota(jnp.int32, (48, 384), 1)
    offs = rows_of(384).astype(jnp.int32)
    landed = column + offs
    offs = jnp.where((landed >= 0) & (landed < 384), offs, 99)

    def sweep(field, top, low, high):
        here = slice(low - top, high - top)
        u = field[here]
        rows = field.shape[0]
        upper = pltpu.roll(field, 4, 0)[here]
        lower = pltpu.roll(field, rows - 4, 0)[here]
        near_off, across = offs[low:high], column[low:high]
        linked = jnp.zeros_like(u)
        for shift in range(-3, 4):
            moved = lower if shift == 0 else pltpu.roll(lower, (-shift) % 384, 1)
            linked = jnp.where(near_off == shift, moved, linked)
        left = jnp.where(across == 0, 0.0, pltpu.roll(u, 1, 1))
        right = jnp.where(across == 383, 0.0, pltpu.roll(u, 383, 1))
        return u + coef[low:high] * (left + right + upper + linked - 4.0 * u)

    def smooth(field):
        field = sweep(field, 0, 0, 48)
        field = sweep(field, 0, 8, 40)
        field = sweep(field, 8, 8, 40)
        return sweep(field, 8, 16, 32)

    take(spec_buf.at[:, pl.ds(0, NZH - 1)], spec_recv_2)
    mine = pl.ds(pl.multiple_of(lax.div(zc, 8) * 8, 8), 8)
    spec_buf[:, zh] = spec_row[:, mine, :]
    pick = lax.broadcasted_iota(jnp.int32, (32, 8, 128), 1) == lax.rem(zc, 8)
    gathered = jnp.sum(jnp.where(pick, spec_buf[...].reshape(32, 8, 128), 0.0), axis=1)
    lane = lax.broadcasted_iota(jnp.int32, (32, 128), 1)
    sensor_row = lax.broadcasted_iota(jnp.int32, (32, 256), 0)
    sensor_lane = lax.broadcasted_iota(jnp.int32, (32, 256), 1) // 8
    whole = []
    for q in range(8):
        piece = jnp.where(lane // 8 == q, gathered, 0.0)
        for shift in (8, 16, 32, 64):
            piece = piece + pltpu.roll(piece, shift, 1)
        piece = jnp.concatenate([piece, piece], axis=1)
        whole.append(jnp.sum(jnp.where(sensor_row == sensor_lane, piece, 0.0), axis=0, keepdims=True))

    def stack(re, im):
        re, im = re.astype(BF16).astype(F32), im.astype(BF16).astype(F32)
        return jnp.concatenate(
            [jnp.concatenate([re, im], 1), jnp.concatenate([im, -re], 1)], 0
        ).astype(BF16)

    def weights(core, low):
        return w_buf[core, low].reshape(512, 384)

    def adjoint_of(h, spectra):
        for q in range(4):
            halo[h, 1, q] = jnp.dot(spectra, weights(q % 2, q // 2), preferred_element_type=F32)

    def rest_of(h, meanwhile):
        to_neighbours(halo.at[h], halo_send.at[h], halo_recv.at[h])
        done = meanwhile()
        from_neighbours(halo.at[h], halo_recv.at[h])
        parts = [halo[h, b, r] for b in range(3) for r in range(4)]
        smoothed = smooth(jnp.concatenate(parts, axis=0))
        total = jnp.zeros((4, 512), F32)
        for q in range(4):
            prior = smoothed[4 * q : 4 * q + 4].astype(BF16)
            total = total + dot_rows(prior, weights(q % 2, q // 2))
        sums[h, x] = jnp.concatenate(
            [total[0:2, :256] - total[2:4, 256:], total[2:4, :256] + total[0:2, 256:]], 0
        )
        for dx in range(1, NX):
            remote(sums.at[h, x], sums.at[h, x], sum_send.at[h], sum_recv.at[h], in_x(dx))
        take(sums.at[h, pl.ds(0, NX - 1)], sum_recv.at[h])
        forward = ((sums[h, 0] + sums[h, 1]) + sums[h, 2]) + sums[h, 3]
        return forward, done

    def arrange(forward, rows, first):
        for q in range(4):
            piece = jnp.where(sensor_row == sensor_lane, jnp.broadcast_to(forward[q : q + 1], (32, 256)), 0.0)
            piece = piece[:, :128] + piece[:, 128:]
            for shift in (8, 16, 32, 64):
                piece = piece + pltpu.roll(piece, shift, 1)
            rows = jnp.where(lane // 8 == (q // 2) * 4 + first + q % 2, piece, rows)
        return rows

    def send_outs(rows):
        out_own[...] = rows.reshape(NY, NZH, 1, 128)

        mine = out_buf.at[y * 16 + zc]
        for dz in (2, 1, 3, 0):
            zh2 = wrap(zh + dz, NZH)

            def send_block(k, y2):
                for q2 in range(4):
                    remote(out_own.at[y2, zh2], mine, out_send, out_recv, dev(y2, zh2, q2))
                return wrap(y2 + 1, NY)

            lax.fori_loop(0, NY if dz else NY - 1, send_block, in_y(4 if dz else 1))
        for dq in range(1, 4):
            remote(out_own.at[y, zh], mine, out_send, out_recv, dev(y, zh, wrap(q_me + dq, 4)))
        out_buf[y * 16 + zc] = out_own[y, zh]

    def backs():
        take(out_buf.at[pl.ds(0, NY * 16 - 1)], out_recv)
        loads[6].wait()
        got = out_buf[...].reshape(128, 128)
        left = jnp.concatenate([got[:, :32], got[:, 32:64]], 0).T
        pieces = []
        for _ in range(3):
            pieces.append(left.astype(BF16))
            left = left - pieces[-1].astype(F32)
        total = jnp.zeros((32, 256), F32)
        for a, b in ((2, 0), (0, 2), (1, 1), (1, 0), (0, 1), (0, 0)):
            total = total + jnp.dot(pieces[a], split_ref[b], preferred_element_type=F32)
        return total[:16], total[16:]

    first = stack(jnp.concatenate(whole[0:2], 0), jnp.concatenate(whole[4:6], 0))
    for copy in kept:
        copy.wait()
    take(whole_b, two_recv.at[0])
    take(whole_a, two_recv.at[1])
    adjoint_of(0, first)
    forward, _ = rest_of(0, lambda: None)
    second = stack(
        jnp.concatenate(whole[2:4], 0) - forward[0:2], jnp.concatenate(whole[6:8], 0) - forward[2:4]
    )
    adjoint_of(1, second)
    forward_1, rows = rest_of(1, lambda: arrange(forward, jnp.zeros((32, 128), F32), 0))
    send_outs(arrange(forward_1, rows, 2))
    back_0, back_1 = backs()
    residual = rest - back_0
    res_ref[...] = residual.reshape(2, 8, 256)
    app_ref[...] = (back_1 + noise16 * residual).reshape(2, 8, 256)

    take(whole_a, one_send.at[0])
    take(whole_b, one_send.at[1])
    take(whole_b, two_send.at[0])
    take(whole_a, two_send.at[1])
    take(spec_row.at[pl.ds(0, NY - 1)], spec_send)
    take(spec_buf.at[:, pl.ds(0, NZH - 1)], spec_send_2)
    take(co_buf.at[1, pl.ds(0, 3)], row_send)
    def sent(buf, send):
        @pl.when(below)
        def _():
            take(buf.at[0], send.at[0])

        @pl.when(above)
        def _():
            take(buf.at[2], send.at[1])

    sent(co_buf, co_send)
    for h in range(2):
        sent(halo.at[h], halo_send.at[h])
        take(sums.at[h, pl.ds(0, NX - 1)], sum_send.at[h])
    take(out_buf.at[pl.ds(0, NY * 16 - 1)], out_send)


def body(vectors, observed, operator, noise, coefficient, offsets):
    rows = basis_rows(vectors.shape[-1])
    vmem = pl.BlockSpec(memory_space=pltpu.VMEM)
    dma = pltpu.SemaphoreType.DMA
    return pl.pallas_call(
        kernel,
        out_shape=(jax.ShapeDtypeStruct(vectors.shape, F32),) * 2,
        in_specs=[pl.BlockSpec(memory_space=pl.ANY)] * 8,
        out_specs=(vmem, vmem),
        scratch_shapes=[
            pltpu.VMEM((2, 8, 256), F32),
            pltpu.VMEM((2, 8, 256), F32),
            pltpu.VMEM((1, 8), F32),
            pltpu.VMEM((1, 384), F32),
            pltpu.VMEM((1, 384), jnp.int32),
            pltpu.VMEM((128, 512), F32),
            pltpu.VMEM((3, 256, 256), BF16),
            pltpu.VMEM((NY, 16, 8, 384), BF16),
            pltpu.VMEM((2, 2, NZH, NY, 8, 384), BF16),
            pltpu.VMEM((2, 2, 2, NY, NZH, 8, 384), BF16),
            pltpu.VMEM((128, 128), F32),
            pltpu.VMEM((NY, 16, 128), F32),
            pltpu.VMEM((NY, NZH, 8, 128), F32),
            pltpu.VMEM((3, 4, 1, 768), F32),
            pltpu.VMEM((2, 3, 4, 4, 384), F32),
            pltpu.VMEM((2, 4, 4, 256), F32),
            pltpu.VMEM((NY, NZH, 1, 128), F32),
            pltpu.VMEM((NY * 16, 1, 128), F32),
            dma((7,)), dma((2,)), dma((2,)), dma((2, 2)), dma((2,)), dma((2,)),
            dma, dma, dma, dma, dma, dma, dma((2,)), dma((2,)),
            dma((2, 2)), dma((2, 2)), dma((2,)), dma((2,)), dma, dma,
        ],
        compiler_params=pltpu.CompilerParams(
            collective_id=0, has_side_effects=True, vmem_limit_bytes=60 * 1024 * 1024
        ),
    )(vectors, observed, operator.reshape(2, NY, 16, 8, 384), noise.reshape(1, 8), coefficient, offsets, jnp.asarray(rows), jnp.asarray(basis_split(rows)))


def solution(mesh):
    placed = (
        P(None, "sen", None),
        P(None, "sen", None),
        P(None, None, "sen", "par"),
        P("sen"),
        P("par", None),
        P("par", None),
    )
    return jax.shard_map(
        body,
        mesh=mesh,
        in_specs=placed,
        out_specs=(P(None, "sen", None), P(None, "sen", None)),
        check_vma=False,
    )
```

```python
import math

import jax
import jax.numpy as jnp
import numpy as np
from jax import lax
from jax.experimental import pallas as pl
from jax.experimental.pallas import tpu as pltpu
from jax.sharding import PartitionSpec as P

SWEEPS = 4
NY, NZH, NX, NZL = 8, 4, 4, 2
NZ = NZH * NZL
F32, BF16 = jnp.float32, jnp.bfloat16


def basis_rows(length):
    half = length // 2
    freqs = np.arange(half)[:, None]
    times = np.arange(length)[None, :]
    angle = ((2 * freqs + 1) * times % (2 * length)) * (math.pi / length)
    scale = math.sqrt(2.0 / length)
    return np.concatenate([np.cos(angle) * scale, np.sin(angle) * scale], 1).astype(np.float32)


def basis_split(rows):
    rest = np.concatenate(np.split(rows, 2, axis=1), 0)
    pieces = []
    for _ in range(3):
        pieces.append(rest.astype(BF16))
        rest = rest - pieces[-1].astype(np.float32)
    return np.stack(pieces)


def dot_rows(a, b, **kw):
    return lax.dot_general(a, b, (((1,), (1,)), ((), ())), preferred_element_type=F32, **kw)


def kernel(
    vec_hbm, obs_hbm, op_ref, noise_hbm, coef_hbm, offs_hbm, basis_hbm, split_hbm,
    out_ref,
    vec_ref, obs_ref, noise_ref, coef_ref, offs_ref, basis_ref, split_ref,
    a_buf, b_buf, w_buf, spec_own, spec_row, spec_buf, co_buf, halo, sums, out_own, out_buf,
    load_sem, op_local, one_send, one_recv, two_send, two_recv,
    spec_send, spec_recv, spec_send_2, spec_recv_2, row_send, row_recv, co_send, co_recv,
    halo_send, halo_recv, sum_send, sum_recv, out_send, out_recv,
):
    sen = lax.axis_index("sen")
    par = lax.axis_index("par")
    x, q_me = lax.div(par, 4), lax.rem(par, 4)
    zl, c = lax.div(q_me, 2), lax.rem(q_me, 2)

    def wrap(value, size):
        return jnp.where(value >= size, value - size, value)

    def at(sen2, par2):
        return sen2 * (4 * NX) + par2

    def in_x(dx):
        return at(sen, wrap(x + dx, NX) * 4 + q_me)

    y, zh = lax.div(sen, NZH), lax.rem(sen, NZH)
    zc = zh * 4 + q_me
    far_y = (4, 3, 5, 2, 6, 1, 7)
    far_z = [(dz, dq) for dz in (2, 1, 3, 0) for dq in range(4) if dz or dq]

    def dev(y2, zh2, q2):
        return at(y2 * NZH + zh2, x * 4 + q2)

    def in_y(dy):
        return wrap(y + dy, NY)

    def in_z(dz, dq):
        return wrap(zh + dz, NZH), wrap(q_me + dq, 4)

    def remote(src, dst, send, recv, device):
        copy = pltpu.make_async_remote_copy(
            src_ref=src, dst_ref=dst, send_sem=send, recv_sem=recv,
            device_id=device, device_id_type=pl.DeviceIdType.LOGICAL,
        )
        copy.start()

    def take(ref, sem):
        pltpu.make_async_copy(ref, ref, sem).wait()

    barrier = pltpu.get_barrier_semaphore()

    def tell(device):
        pl.semaphore_signal(barrier, inc=1, device_id=device, device_id_type=pl.DeviceIdType.LOGICAL)

    for dy in far_y:
        tell(dev(in_y(dy), zh, q_me))
    for dz, dq in far_z:
        tell(dev(y, *in_z(dz, dq)))
    for dx in range(1, NX):
        tell(in_x(dx))

    loads = []
    for i, (src, dst) in enumerate(
        ((vec_hbm, vec_ref), (obs_hbm, obs_ref), (noise_hbm, noise_ref),
         (coef_hbm, coef_ref), (offs_hbm, offs_ref), (basis_hbm, basis_ref), (split_hbm, split_ref))
    ):
        loads.append(pltpu.make_async_copy(src, dst, load_sem.at[i]))
        loads[-1].start()

    own = [
        pltpu.make_async_copy(op_ref.at[0, y], a_buf.at[y], op_local.at[0]),
        pltpu.make_async_copy(op_ref.at[1, :, zc], b_buf.at[c, zl, zh], op_local.at[1]),
    ]
    for copy in own:
        copy.start()

    pl.semaphore_wait(barrier, 22 + NX - 1)

    half_y, half_z = lax.div(y, 4), lax.div(zh, 2)

    def first_stage(sub):
        to_y = 1 - half_y if sub == 0 else half_y
        to_z = 1 - half_z if sub == 0 else half_z
        cut_y = pl.ds(to_y * 4, 4)
        cut_z = pl.ds(to_z * 8, 8)
        for n, (dz, dq) in enumerate(far_z):
            if n % 2 == 0 and n // 2 < 7:
                y2 = in_y(far_y[n // 2])
                remote(
                    op_ref.at[0, y2, cut_z], a_buf.at[y, cut_z],
                    one_send.at[0], one_recv.at[0, sub], dev(y2, zh, q_me),
                )
            zh2, q2 = in_z(dz, dq)
            remote(
                op_ref.at[1, cut_y, zh2 * 4 + q2], b_buf.at[c, zl, zh, cut_y],
                one_send.at[1], one_recv.at[1, sub], dev(y, zh2, q2),
            )

    first_stage(0)

    for load in loads[:6]:
        load.wait()
    eye = lax.broadcasted_iota(jnp.int32, (8, 8), 0) == lax.broadcasted_iota(jnp.int32, (8, 8), 1)
    noise = jnp.sum(jnp.where(eye, noise_ref[...], 0.0), axis=1, keepdims=True)
    noise16 = jnp.concatenate([noise, noise], axis=0)
    vec = vec_ref[...].reshape(16, 256)
    rest = obs_ref[...].reshape(16, 256) - noise16 * vec
    record = jnp.concatenate([vec, rest], axis=0)
    blank = jnp.zeros_like(record)
    both = jnp.concatenate(
        [jnp.concatenate([record, blank], 1), jnp.concatenate([blank, record], 1), jnp.zeros((64, 512), F32)], 0
    )
    spec_own[...] = dot_rows(basis_ref[...], both, precision=lax.Precision.HIGHEST)

    co_buf[1, q_me, :, 0:384] = coef_ref[...]
    co_buf[1, q_me, :, 384:768] = offs_ref[...].astype(F32)

    for dy in far_y:
        y2 = in_y(dy)
        rows = pl.ds(pl.multiple_of(y2 * 16, 16), 16)
        remote(spec_own.at[rows], spec_row.at[y], spec_send, spec_recv, dev(y2, zh, q_me))
    for dq in range(1, 4):
        remote(co_buf.at[1, q_me], co_buf.at[1, q_me], row_send, row_recv, dev(y, zh, wrap(q_me + dq, 4)))

    first_stage(1)

    take(co_buf.at[1, pl.ds(0, 3)], row_recv)
    above, below = x > 0, x < NX - 1

    def to_neighbours(buf, send, recv):
        @pl.when(below)
        def _():
            remote(buf.at[1], buf.at[0], send.at[0], recv.at[0], par_at(x + 1))

        @pl.when(above)
        def _():
            remote(buf.at[1], buf.at[2], send.at[1], recv.at[1], par_at(x - 1))

    def from_neighbours(buf, recv):
        @pl.when(above)
        def _():
            take(buf.at[0], recv.at[0])

        @pl.when(below)
        def _():
            take(buf.at[2], recv.at[1])

    def par_at(x2):
        return at(sen, x2 * 4 + q_me)

    def clear(buf):
        @pl.when(x == 0)
        def _():
            buf[0] = jnp.zeros(buf.shape[1:], F32)

        @pl.when(x == NX - 1)
        def _():
            buf[2] = jnp.zeros(buf.shape[1:], F32)

    clear(co_buf)
    for h in range(2):
        clear(halo.at[h])
    to_neighbours(co_buf, co_send, co_recv)

    take(spec_row.at[pl.ds(0, NY - 1)], spec_recv)
    spec_row[y] = spec_own[pl.ds(pl.multiple_of(y * 16, 16), 16), :]
    for dz in range(1, NZH):
        zh2 = wrap(zh + dz, NZH)
        rows = pl.ds(pl.multiple_of(lax.div(zh2, 2) * 8, 8), 8)
        remote(spec_row.at[:, rows], spec_buf.at[:, zh], spec_send_2, spec_recv_2, dev(y, zh2, q_me))

    def send_z(zh2, q2):
        remote(
            a_buf.at[:, zh2 * 4 + q2], w_buf.at[c, zl, 0, :, zh], two_send.at[0], two_recv.at[0], dev(y, zh2, q2)
        )

    def send_y(y2):
        remote(b_buf.at[:, :, :, y2], w_buf.at[:, :, 1, y], two_send.at[1], two_recv.at[1], dev(y2, zh, q_me))

    half_a = op_ref.at[0, pl.ds(0, NY - 1), pl.ds(0, 8)]
    half_b = op_ref.at[0, pl.ds(0, 4), pl.ds(0, 15)]
    whole_a = op_ref.at[0, pl.ds(0, NY - 1)]
    whole_b = op_ref.at[0, :, pl.ds(0, 15)]
    for copy in own:
        copy.wait()
    take(half_a, one_recv.at[0, 0])
    for low in range(2):
        for q2 in range(4):
            send_z((1 - half_z) * 2 + low, q2)
    take(half_b, one_recv.at[1, 0])
    for low in range(4):
        send_y((1 - half_y) * 4 + low)
    take(half_a, one_recv.at[0, 1])
    for q2 in range(4):
        send_z(half_z * 4 + 1 - zh, q2)
    for dq in range(1, 4):
        send_z(zh, wrap(q_me + dq, 4))
    take(half_b, one_recv.at[1, 1])
    for dy in range(1, 4):
        send_y(half_y * 4 + wrap(y - half_y * 4 + dy, 4))
    kept = [
        pltpu.make_async_copy(a_buf.at[:, zc], w_buf.at[c, zl, 0, :, zh], op_local.at[0]),
        pltpu.make_async_copy(b_buf.at[:, :, :, y], w_buf.at[:, :, 1, y], op_local.at[1]),
    ]
    for copy in kept:
        copy.start()

    from_neighbours(co_buf, co_recv)

    def rows_of(first):
        parts = []
        for b in range(3):
            for r in range(4):
                parts.append(jnp.broadcast_to(co_buf[b, r, :, first : first + 384], (4, 384)))
        return jnp.concatenate(parts, axis=0)

    coef = rows_of(0)
    column = lax.broadcasted_iota(jnp.int32, (48, 384), 1)
    offs = rows_of(384).astype(jnp.int32)
    landed = column + offs
    offs = jnp.where((landed >= 0) & (landed < 384), offs, 99)

    def sweep(field, top, low, high):
        here = slice(low - top, high - top)
        u = field[here]
        rows = field.shape[0]
        upper = pltpu.roll(field, 4, 0)[here]
        lower = pltpu.roll(field, rows - 4, 0)[here]
        near_off, across = offs[low:high], column[low:high]
        linked = jnp.zeros_like(u)
        for shift in range(-3, 4):
            moved = lower if shift == 0 else pltpu.roll(lower, (-shift) % 384, 1)
            linked = jnp.where(near_off == shift, moved, linked)
        left = jnp.where(across == 0, 0.0, pltpu.roll(u, 1, 1))
        right = jnp.where(across == 383, 0.0, pltpu.roll(u, 383, 1))
        return u + coef[low:high] * (left + right + upper + linked - 4.0 * u)

    def smooth(field):
        field = sweep(field, 0, 0, 48)
        field = sweep(field, 0, 8, 40)
        field = sweep(field, 8, 8, 40)
        return sweep(field, 8, 16, 32)

    take(spec_buf.at[:, pl.ds(0, NZH - 1)], spec_recv_2)
    mine = pl.ds(pl.multiple_of(lax.div(zc, 8) * 8, 8), 8)
    spec_buf[:, zh] = spec_row[:, mine, :]
    pick = lax.broadcasted_iota(jnp.int32, (32, 8, 128), 1) == lax.rem(zc, 8)
    gathered = jnp.sum(jnp.where(pick, spec_buf[...].reshape(32, 8, 128), 0.0), axis=1)
    lane = lax.broadcasted_iota(jnp.int32, (32, 128), 1)
    sensor_row = lax.broadcasted_iota(jnp.int32, (32, 256), 0)
    sensor_lane = lax.broadcasted_iota(jnp.int32, (32, 256), 1) // 8
    whole = []
    for q in range(8):
        piece = jnp.where(lane // 8 == q, gathered, 0.0)
        for shift in (8, 16, 32, 64):
            piece = piece + pltpu.roll(piece, shift, 1)
        piece = jnp.concatenate([piece, piece], axis=1)
        whole.append(jnp.sum(jnp.where(sensor_row == sensor_lane, piece, 0.0), axis=0, keepdims=True))

    def stack(re, im):
        re, im = re.astype(BF16).astype(F32), im.astype(BF16).astype(F32)
        return jnp.concatenate(
            [jnp.concatenate([re, im], 1), jnp.concatenate([im, -re], 1)], 0
        ).astype(BF16)

    def weights(core, low):
        return w_buf[core, low].reshape(512, 384)

    def adjoint_of(h, spectra):
        for q in range(4):
            halo[h, 1, q] = jnp.dot(spectra, weights(q % 2, q // 2), preferred_element_type=F32)

    def rest_of(h, meanwhile):
        to_neighbours(halo.at[h], halo_send.at[h], halo_recv.at[h])
        done = meanwhile()
        from_neighbours(halo.at[h], halo_recv.at[h])
        parts = [halo[h, b, r] for b in range(3) for r in range(4)]
        smoothed = smooth(jnp.concatenate(parts, axis=0))
        total = jnp.zeros((4, 512), F32)
        for q in range(4):
            prior = smoothed[4 * q : 4 * q + 4].astype(BF16)
            total = total + dot_rows(prior, weights(q % 2, q // 2))
        sums[h, x] = jnp.concatenate(
            [total[0:2, :256] - total[2:4, 256:], total[2:4, :256] + total[0:2, 256:]], 0
        )
        for dx in range(1, NX):
            remote(sums.at[h, x], sums.at[h, x], sum_send.at[h], sum_recv.at[h], in_x(dx))
        take(sums.at[h, pl.ds(0, NX - 1)], sum_recv.at[h])
        forward = ((sums[h, 0] + sums[h, 1]) + sums[h, 2]) + sums[h, 3]
        return forward, done

    def arrange(forward, rows, first):
        for q in range(4):
            piece = jnp.where(sensor_row == sensor_lane, jnp.broadcast_to(forward[q : q + 1], (32, 256)), 0.0)
            piece = piece[:, :128] + piece[:, 128:]
            for shift in (8, 16, 32, 64):
                piece = piece + pltpu.roll(piece, shift, 1)
            rows = jnp.where(lane // 8 == (q // 2) * 4 + first + q % 2, piece, rows)
        return rows

    def send_outs(rows):
        out_own[...] = rows.reshape(NY, NZH, 1, 128)

        mine = out_buf.at[y * 16 + zc]
        for dz in (2, 1, 3, 0):
            zh2 = wrap(zh + dz, NZH)

            def send_block(k, y2):
                for q2 in range(4):
                    remote(out_own.at[y2, zh2], mine, out_send, out_recv, dev(y2, zh2, q2))
                return wrap(y2 + 1, NY)

            y2 = in_y(4 if dz else 1)
            for k in range(NY if dz else NY - 1):
                y2 = send_block(k, y2)
        for dq in range(1, 4):
            remote(out_own.at[y, zh], mine, out_send, out_recv, dev(y, zh, wrap(q_me + dq, 4)))
        out_buf[y * 16 + zc] = out_own[y, zh]

    def backs():
        take(out_buf.at[pl.ds(0, NY * 16 - 1)], out_recv)
        loads[6].wait()
        got = out_buf[...].reshape(128, 128)
        left = jnp.concatenate([got[:, :32], got[:, 32:64]], 0).T
        pieces = []
        for _ in range(3):
            pieces.append(left.astype(BF16))
            left = left - pieces[-1].astype(F32)
        total = jnp.zeros((32, 256), F32)
        for a, b in ((2, 0), (0, 2), (1, 1), (1, 0), (0, 1), (0, 0)):
            total = total + jnp.dot(pieces[a], split_ref[b], preferred_element_type=F32)
        return total[:16], total[16:]

    first = stack(jnp.concatenate(whole[0:2], 0), jnp.concatenate(whole[4:6], 0))
    for copy in kept:
        copy.wait()
    take(whole_b, two_recv.at[0])
    take(whole_a, two_recv.at[1])
    adjoint_of(0, first)
    forward, _ = rest_of(0, lambda: None)
    second = stack(
        jnp.concatenate(whole[2:4], 0) - forward[0:2], jnp.concatenate(whole[6:8], 0) - forward[2:4]
    )
    adjoint_of(1, second)
    forward_1, rows = rest_of(1, lambda: arrange(forward, jnp.zeros((32, 128), F32), 0))
    send_outs(arrange(forward_1, rows, 2))
    back_0, back_1 = backs()
    residual = rest - back_0
    out_ref[0] = residual.reshape(2, 8, 256)
    out_ref[1] = (back_1 + noise16 * residual).reshape(2, 8, 256)

    take(whole_a, one_send.at[0])
    take(whole_b, one_send.at[1])
    take(whole_b, two_send.at[0])
    take(whole_a, two_send.at[1])
    take(spec_row.at[pl.ds(0, NY - 1)], spec_send)
    take(spec_buf.at[:, pl.ds(0, NZH - 1)], spec_send_2)
    take(co_buf.at[1, pl.ds(0, 3)], row_send)
    def sent(buf, send):
        @pl.when(below)
        def _():
            take(buf.at[0], send.at[0])

        @pl.when(above)
        def _():
            take(buf.at[2], send.at[1])

    sent(co_buf, co_send)
    for h in range(2):
        sent(halo.at[h], halo_send.at[h])
        take(sums.at[h, pl.ds(0, NX - 1)], sum_send.at[h])
    take(out_buf.at[pl.ds(0, NY * 16 - 1)], out_send)


def body(vectors, observed, operator, noise, coefficient, offsets):
    rows = basis_rows(vectors.shape[-1])
    vmem = pl.BlockSpec(memory_space=pltpu.VMEM)
    dma = pltpu.SemaphoreType.DMA
    both = pl.pallas_call(
        kernel,
        out_shape=jax.ShapeDtypeStruct((2, *vectors.shape), F32),
        in_specs=[pl.BlockSpec(memory_space=pl.ANY)] * 8,
        out_specs=vmem,
        scratch_shapes=[
            pltpu.VMEM((2, 8, 256), F32),
            pltpu.VMEM((2, 8, 256), F32),
            pltpu.VMEM((1, 8), F32),
            pltpu.VMEM((1, 384), F32),
            pltpu.VMEM((1, 384), jnp.int32),
            pltpu.VMEM((128, 512), F32),
            pltpu.VMEM((3, 256, 256), BF16),
            pltpu.VMEM((NY, 16, 8, 384), BF16),
            pltpu.VMEM((2, 2, NZH, NY, 8, 384), BF16),
            pltpu.VMEM((2, 2, 2, NY, NZH, 8, 384), BF16),
            pltpu.VMEM((128, 128), F32),
            pltpu.VMEM((NY, 16, 128), F32),
            pltpu.VMEM((NY, NZH, 8, 128), F32),
            pltpu.VMEM((3, 4, 1, 768), F32),
            pltpu.VMEM((2, 3, 4, 4, 384), F32),
            pltpu.VMEM((2, 4, 4, 256), F32),
            pltpu.VMEM((NY, NZH, 1, 128), F32),
            pltpu.VMEM((NY * 16, 1, 128), F32),
            dma((7,)), dma((2,)), dma((2,)), dma((2, 2)), dma((2,)), dma((2,)),
            dma, dma, dma, dma, dma, dma, dma((2,)), dma((2,)),
            dma((2, 2)), dma((2, 2)), dma((2,)), dma((2,)), dma, dma,
        ],
        compiler_params=pltpu.CompilerParams(
            collective_id=0, has_side_effects=True, vmem_limit_bytes=60 * 1024 * 1024
        ),
    )(vectors, observed, operator.reshape(2, NY, 16, 8, 384), noise.reshape(1, 8), coefficient, offsets, jnp.asarray(rows), jnp.asarray(basis_split(rows)))
    return both[0], both[1]


def solution(mesh):
    placed = (
        P(None, "sen", None),
        P(None, "sen", None),
        P(None, None, "sen", "par"),
        P("sen"),
        P("par", None),
        P("par", None),
    )
    return jax.shard_map(
        body,
        mesh=mesh,
        in_specs=placed,
        out_specs=(P(None, "sen", None), P(None, "sen", None)),
        check_vma=False,
    )
```
